32 devices in a mesh: group: 2 (over y), mid: 4 (over z), freq: 2 (over x), off: 2 (over core).
Axes of the slice: x: 2, y: 2, z: 4, core: 2. Of those that a mesh axis runs over, the one named last changes fastest.
Arguments:
- traces: bfloat16 [2, 1024, 1024], P('off', ('group', 'mid', 'freq')), parts along dimension 1, may hold values from -6 to 6
- time_filter: bfloat16 [1024, 1024], replicated, may hold values from -0.1875 to 0.1875
- midpoint_of: int32 [2, 1024], P('off', 'group'), parts along dimension 1, may hold values from 0 to 7, as said below
- offset_of: int32 [2, 1024], P('off', 'group'), parts along dimension 1, may hold values from 0 to 127, as said below
- shrink_level: float32 [512], P('freq'), may hold values from 0.2 to 2
Outputs:
- primaries: bfloat16 [2, 1024, 1024], P('off', ('group', 'mid', 'freq')), parts along dimension 1
The draws below stay inside these ranges and needn't reach their ends.
There are 2 independent parts, one for each index of `group`. The reference program is written for one: setup_inputs(seed, part) draws one part's arguments, and reference() takes and returns one part's arrays. A program takes and returns all parts, laid end to end along the dimension named above; an argument that names none is the same for every part. Nothing has to cross between parts.
Inputs may be any that keep to these rules, and one draw needn't show every extreme that they name: `midpoint_of`: together with offset_of, every (midpoint, offset) pair occurs exactly once in a part; the traces of one device (a block of 64 along the second dimension) go to midpoint owners (midpoint // 2) in counts of 32 for a quarter of the owners, 16 for another quarter and 8 for the rest, so at most 32 traces from one device reach one owner. `offset_of`: traces at first index o have offsets in o * 64 up to (o + 1) * 64 - 1.
All inputs are finite; a program needn't handle non-finite values.
Results may differ from the reference program's by a relative error of at most 0.0076.
Values may be sent and summed in bfloat16 or wider, within the bound.
A program may use at most 64 MiB of HBM per device.

```python
import math
import jax
import jax.numpy as jnp

NT = 1024
NF = 512
NOFF = 128
NP = 128
TR_DEV = 64
NCMP = 8
TRH = 512
N_MID = 4
N_FREQ = 2
N_OFF = 2


def geometry(key):
    base_key = jax.random.fold_in(key, 11)
    quota_rows = TR_DEV // N_MID
    noff_dev = NOFF // N_OFF
    cmp_dev = N_FREQ * TR_DEV // noff_dev
    owners = jnp.arange(N_MID, dtype=jnp.int32)
    profile = jnp.where(owners < N_MID // 4, 2 * quota_rows, jnp.where(owners < N_MID // 2, quota_rows, quota_rows // 2))
    bounds = jnp.cumsum(profile)
    places = jnp.arange(TR_DEV, dtype=jnp.int32)
    step_of = jnp.sum((places[:, None] >= bounds[None, :]).astype(jnp.int32), axis=1)
    senders = jnp.arange(N_MID * N_FREQ, dtype=jnp.int32)
    sender_mid = senders // N_FREQ
    sender_freq = senders % N_FREQ
    mid_rows = []
    off_rows = []
    for half_index in range(N_OFF):
        half_key = jax.random.fold_in(base_key, half_index)
        shifts = jax.random.randint(jax.random.fold_in(half_key, 1), (N_FREQ,), 0, N_MID)
        order_keys = jax.random.split(jax.random.fold_in(half_key, 2), N_MID * N_FREQ)
        orders = jax.vmap(lambda sub_key: jax.random.permutation(sub_key, TR_DEV))(order_keys)
        destination = (sender_mid[:, None] + shifts[sender_freq][:, None] + step_of[orders]) % N_MID
        flat_dest = destination.reshape(-1)
        onehot = (flat_dest[:, None] == owners[None, :]).astype(jnp.int32)
        rank_in = jnp.sum(jnp.cumsum(onehot, axis=0) * onehot, axis=1) - 1
        cell_keys = jax.random.split(jax.random.fold_in(half_key, 3), N_MID)
        cell_perm = jax.vmap(lambda sub_key: jax.random.permutation(sub_key, cmp_dev * noff_dev))(cell_keys)
        cell_pick = cell_perm[flat_dest, rank_in].astype(jnp.int32)
        mid_rows.append((flat_dest * cmp_dev + cell_pick // noff_dev).astype(jnp.int32))
        off_rows.append((half_index * noff_dev + cell_pick % noff_dev).astype(jnp.int32))
    return (jnp.stack(mid_rows), jnp.stack(off_rows))


def draw_midpoint_of(key, part):
    return geometry(key)[0]


def draw_offset_of(key, part):
    return geometry(key)[1]


def block_levels(rng, extent, pieces, low, high):
    def one(axis_at, blocks):
        heights = jax.random.uniform(jax.random.fold_in(jax.random.fold_in(rng, 6), axis_at), (blocks,), jnp.float32, low / len(pieces), high / len(pieces))
        return jnp.repeat(jnp.exp(heights), extent[axis_at] // blocks).reshape((-1,) + (1,) * (len(extent) - axis_at - 1))

    factor_of = one(*pieces[0])
    for cut in pieces[1:]:
        factor_of = factor_of * one(*cut)
    return factor_of


def noise(rng, dims, width, limit, cuts=(), kind=jnp.bfloat16):
    gain = block_levels(rng, dims, cuts, -0.22, 0.18) if cuts else 1.0
    values = jax.random.normal(rng, dims, jnp.float32) * width * gain
    return jnp.minimum(jnp.maximum(values, -limit), limit).astype(kind)


def setup_inputs(seed: int = 0, part: int = 0) -> dict:
    keys = jax.random.split(jax.random.key(seed), 6)
    part_keys = jax.random.split(jax.random.fold_in(keys[5], part), 6)
    return {
        "traces": noise(part_keys[0], (N_OFF, TRH, NT), 1.0, 6.0, ((0, 2), (1, 8))),
        "time_filter": noise(keys[1], (NT, NT), NT ** -0.5, 0.1875),
        "midpoint_of": draw_midpoint_of(jax.random.fold_in(jax.random.fold_in(keys[5], part), 71), part),
        "offset_of": draw_offset_of(jax.random.fold_in(jax.random.fold_in(keys[5], part), 71), part),
        "shrink_level": jnp.clip(jnp.exp(math.log(2.0) - 2.3025851 * jax.random.uniform(keys[4], (NF,), jnp.float32) ** block_levels(keys[4], (NF,), ((0, 2),), -0.2, 0.2)), 0.2, 2.0),
    }


two_pi = 2.0 * math.pi
radon_period = 4096

def dft_tables():
    sample = jnp.arange(NT, dtype=jnp.int32)[:, None]
    freq_index = jnp.arange(NF, dtype=jnp.int32)[None, :]
    angle = two_pi * (sample * freq_index % NT).astype(jnp.float32) / NT
    scale_f = 1.0 / math.sqrt(NT)
    cosine = (jnp.cos(angle) * scale_f).astype(jnp.bfloat16)
    sine = (-jnp.sin(angle) * scale_f).astype(jnp.bfloat16)
    return (cosine, sine)

def radon_tables():
    freq_index = jnp.arange(NF, dtype=jnp.int32)[:, None, None]
    offset_index = jnp.arange(NOFF, dtype=jnp.int32)[None, :, None]
    slowness = jnp.arange(NP, dtype=jnp.int32)[None, None, :]
    turns = freq_index * slowness % radon_period * (offset_index * offset_index % radon_period) % radon_period
    angle = two_pi * turns.astype(jnp.float32) / radon_period
    scale_r = 1.0 / math.sqrt(NOFF)
    return ((jnp.cos(angle) * scale_r).astype(jnp.bfloat16), (jnp.sin(angle) * scale_r).astype(jnp.bfloat16))

def smooth_edges(grid):
    padded = jnp.pad(grid.astype(jnp.float32), ((1, 1), (0, 0), (0, 0)))
    return ((padded[:-2] + 2.0 * padded[1:-1] + padded[2:]) * 0.25).astype(jnp.bfloat16)

def reference(traces, time_filter, midpoint_of, offset_of, shrink_level):
    flat_traces = traces.reshape(-1, NT)
    filtered = jnp.dot(flat_traces, time_filter, preferred_element_type=jnp.float32).astype(jnp.bfloat16)
    cos_tab, sin_tab = dft_tables()
    spec_re = jnp.dot(filtered, cos_tab, preferred_element_type=jnp.float32).astype(jnp.bfloat16)
    spec_im = jnp.dot(filtered, sin_tab, preferred_element_type=jnp.float32).astype(jnp.bfloat16)
    mids = midpoint_of.reshape(-1)
    offs = offset_of.reshape(-1)
    gather_re = jnp.zeros((NCMP, NOFF, NF), spec_re.dtype).at[mids, offs].set(spec_re)
    gather_im = jnp.zeros((NCMP, NOFF, NF), spec_im.dtype).at[mids, offs].set(spec_im)
    smooth_re = smooth_edges(gather_re).astype(jnp.float32)
    smooth_im = smooth_edges(gather_im).astype(jnp.float32)
    rad_cos, rad_sin = radon_tables()
    rad_cos = rad_cos.astype(jnp.float32)
    rad_sin = rad_sin.astype(jnp.float32)
    model_re = jnp.einsum('chk,khp->ckp', smooth_re, rad_cos) - jnp.einsum('chk,khp->ckp', smooth_im, rad_sin)
    model_im = jnp.einsum('chk,khp->ckp', smooth_re, rad_sin) + jnp.einsum('chk,khp->ckp', smooth_im, rad_cos)
    power = model_re * model_re + model_im * model_im
    levels = shrink_level[None, :, None]
    mask_p = (jnp.arange(NP) >= NP // 4).astype(jnp.float32)
    factor = power / (power + levels * levels) * mask_p
    kept_re = (model_re * factor).astype(jnp.bfloat16).astype(jnp.float32)
    kept_im = (model_im * factor).astype(jnp.bfloat16).astype(jnp.float32)
    mult_re = jnp.einsum('ckp,khp->chk', kept_re, rad_cos) + jnp.einsum('ckp,khp->chk', kept_im, rad_sin)
    mult_im = jnp.einsum('ckp,khp->chk', kept_im, rad_cos) - jnp.einsum('ckp,khp->chk', kept_re, rad_sin)
    clean_re = (gather_re.astype(jnp.float32) - mult_re).astype(jnp.bfloat16)
    clean_im = (gather_im.astype(jnp.float32) - mult_im).astype(jnp.bfloat16)
    back_re = clean_re[mids, offs]
    back_im = clean_im[mids, offs]
    total = jnp.dot(back_re, cos_tab.T, preferred_element_type=jnp.float32) + jnp.dot(back_im, sin_tab.T, preferred_element_type=jnp.float32)
    return (2.0 * total).astype(jnp.bfloat16).reshape(N_OFF, TRH, NT)
```

```python
import functools
import math

import jax
import jax.numpy as jnp
import numpy as np
from jax import lax
from jax.experimental import pallas as pl
from jax.experimental.pallas import tpu as pltpu
from jax.sharding import PartitionSpec as P

NOFF = 128
NP = 128
radon_period = 4096
VMEM = pl.BlockSpec(memory_space=pltpu.VMEM)
ANY = pl.BlockSpec(memory_space=pl.ANY)


def dft_table(n_time, n_bands, band_size):
    sample = np.arange(n_time, dtype=np.int64)[:, None]
    freq_index = np.arange(n_bands * band_size, dtype=np.int64)[None, :]
    angle = 2.0 * np.pi * (sample * freq_index % n_time) / n_time
    scale_f = 1.0 / math.sqrt(n_time)
    cosine = (np.cos(angle) * scale_f).reshape(n_time, n_bands, band_size)
    sine = (-np.sin(angle) * scale_f).reshape(n_time, n_bands, band_size)
    table = np.stack([cosine, sine], axis=2).reshape(n_time, n_bands * 2 * band_size)
    return table.astype(np.float32).astype(jnp.bfloat16)


def radon_table(n_freqs):
    freq_index = np.arange(n_freqs, dtype=np.int64)[:, None, None]
    offset_index = np.arange(NOFF, dtype=np.int64)[None, :, None]
    slowness = np.arange(NP, dtype=np.int64)[None, None, :]
    turns = freq_index * slowness % radon_period * (offset_index * offset_index % radon_period) % radon_period
    circle = 2.0 * np.pi * np.arange(radon_period) / radon_period
    scale_r = 1.0 / math.sqrt(NOFF)
    cosine = (np.cos(circle) * scale_r).astype(np.float32).astype(jnp.bfloat16)[turns]
    sine = (np.sin(circle) * scale_r).astype(np.float32).astype(jnp.bfloat16)[turns]
    return np.stack([cosine, sine], axis=1).reshape(n_freqs, 2 * NOFF, NP)


def signal(barrier, **device):
    pl.semaphore_signal(barrier, inc=1, device_id=device, device_id_type=pl.DeviceIdType.MESH)


def send(src, dst, send_sem, recv_sem, **device):
    return pltpu.make_async_remote_copy(
        src_ref=src,
        dst_ref=dst,
        send_sem=send_sem,
        recv_sem=recv_sem,
        device_id=device,
        device_id_type=pl.DeviceIdType.MESH,
    )


def place(sizes):
    names = ("off", "mid", "freq")
    here = [lax.axis_index(name) for name in names]
    index = (here[0] * sizes[1] + here[1]) * sizes[2] + here[2]
    total = sizes[0] * sizes[1] * sizes[2]

    def ahead(i):
        there = (index + i) % total
        return there, dict(off=there // (sizes[1] * sizes[2]), mid=there // sizes[2] % sizes[1], freq=there % sizes[2])

    return index, total, ahead


def swap_kernel(sizes, with_ids, *refs):
    if with_ids:
        blocks, ids, got, got_ids, own_sem, send_sem, recv_sem, id_own, id_send, id_recv = refs
    else:
        blocks, got, own_sem, send_sem, recv_sem = refs
    index, total, ahead = place(sizes)
    n_off = sizes[0]
    barrier = pltpu.get_barrier_semaphore()

    @pl.loop(1, total)
    def _(i):
        signal(barrier, **ahead(i)[1])

    own = pltpu.make_async_copy(blocks.at[index], got.at[index], own_sem)
    own.start()
    pl.semaphore_wait(barrier, total - 1)

    def block_copy(i):
        there, device = ahead(i)
        return send(blocks.at[there], got.at[index], send_sem.at[i], recv_sem.at[i], **device)

    def id_copy(d):
        off = lax.axis_index("off")
        return send(ids, got_ids.at[off], id_send.at[d], id_recv.at[d], off=(off + d) % n_off)

    if with_ids:
        own_ids = pltpu.make_async_copy(ids, got_ids.at[lax.axis_index("off")], id_own)
        own_ids.start()
        for d in range(1, n_off):
            id_copy(d).start()

    @pl.loop(1, total)
    def _(i):
        block_copy(i).start()

    own.wait()
    if with_ids:
        own_ids.wait()
        for d in range(1, n_off):
            id_copy(d).wait()

    @pl.loop(1, total)
    def _(i):
        block_copy(i).wait()


def swap(blocks, sizes, collective_id, ids=None):
    total, n_off = blocks.shape[0], sizes[0]
    dma = pltpu.SemaphoreType.DMA
    shapes = [jax.ShapeDtypeStruct(blocks.shape, blocks.dtype)]
    scratch = [dma, dma((total,)), dma((total,))]
    operands = [blocks]
    if ids is not None:
        shapes.append(jax.ShapeDtypeStruct((n_off,) + ids.shape, ids.dtype))
        scratch += [dma, dma((n_off,)), dma((n_off,))]
        operands.append(ids)
    return pl.pallas_call(
        functools.partial(swap_kernel, sizes, ids is not None),
        out_shape=shapes,
        in_specs=[VMEM] * len(operands),
        out_specs=[VMEM] * len(shapes),
        scratch_shapes=scratch,
        compiler_params=pltpu.CompilerParams(collective_id=collective_id, has_side_effects=True),
    )(*operands)


def radon_kernel(n_mid, n_off, smooth, level, table, out, weights, sem):
    count, mids = smooth.shape[1:3]
    q = (lax.axis_index("freq") * n_mid + lax.axis_index("mid")) * n_off + lax.axis_index("off")
    fetch = pltpu.make_async_copy(table.at[pl.ds(q * count, count)], weights, sem)
    fetch.start()
    re = smooth[0].astype(jnp.float32)
    im = smooth[1].astype(jnp.float32)
    first = jnp.concatenate([re, -im], axis=2)
    second = jnp.concatenate([im, re], axis=2)
    x = jnp.concatenate([first, second], axis=1).astype(jnp.bfloat16)
    fetch.wait()
    model = lax.dot_general(x, weights[...], (((2,), (1,)), ((0,), (0,))), preferred_element_type=jnp.float32)
    model_re, model_im = model[:, :mids], model[:, mids:]
    power = model_re * model_re + model_im * model_im
    keep = (lax.broadcasted_iota(jnp.int32, power.shape, 2) >= NP // 4).astype(jnp.float32)
    lev = level[...]
    factor = power / (power + lev * lev) * keep
    kept = jnp.concatenate([model_re * factor, model_im * factor], axis=1).astype(jnp.bfloat16)
    both = lax.dot_general(kept, weights[...], (((2,), (2,)), ((0,), (0,))), preferred_element_type=jnp.float32)
    out[0] = (both[:, :mids, :NOFF] + both[:, mids:, NOFF:]).astype(jnp.bfloat16)
    out[1] = (both[:, mids:, :NOFF] - both[:, :mids, NOFF:]).astype(jnp.bfloat16)


def radon(smooth, level, table, n_mid, n_off):
    count = smooth.shape[1]
    return pl.pallas_call(
        functools.partial(radon_kernel, n_mid, n_off),
        out_shape=jax.ShapeDtypeStruct(smooth.shape, jnp.bfloat16),
        in_specs=[VMEM, VMEM, ANY],
        out_specs=VMEM,
        scratch_shapes=[pltpu.VMEM((count, 2 * NOFF, NP), jnp.bfloat16), pltpu.SemaphoreType.DMA],
        compiler_params=pltpu.CompilerParams(vmem_limit_bytes=24 * 1024 * 1024),
    )(smooth, level, table)


def fused_kernel(sizes, traces_hbm, filter_hbm, mid_hbm, off_hbm, level_hbm, dft_hbm, inv_hbm, table_hbm, out, traces, filt, mid_ids, off_ids, level, dft, inv, weights, keys, key_col, near, same, blocks, got, back, ret, routes, cube, lev, load_sem, filt_sem, dft_sem, send_sem, recv_sem, id_send, id_recv):
    n_off, n_mid, n_freq = sizes
    total = n_off * n_mid * n_freq
    off, mid, freq = (lax.axis_index(name) for name in ("off", "mid", "freq"))
    f32, bf16 = jnp.float32, jnp.bfloat16
    lines, wide = blocks.shape[1:]
    width = wide // 2
    count = width // 2
    half = NOFF // n_off
    mids = lev.shape[1]
    cells = mids * half
    per_half = keys.shape[2]
    spacing = 2 * mids
    group = n_off * n_freq * width

    def peer(dm, df, do):
        m, f, o = lax.rem(mid + dm, n_mid), lax.rem(freq + df, n_freq), lax.rem(off + do, n_off)
        return (o * n_mid + m) * n_freq + f, dict(off=o, mid=m, freq=f)

    index = (off * n_mid + mid) * n_freq + freq
    far_first = sorted(range(n_mid), key=lambda dm: (dm == 0, abs(dm - n_mid // 2)))
    peers = [(dm, df, do) for dm in far_first for df in reversed(range(n_freq)) for do in reversed(range(n_off))]
    slot = {p: i for i, p in enumerate(peers)}
    others = [p for p in peers if p != (0, 0, 0)]
    barrier = pltpu.get_barrier_semaphore()
    for p in others:
        signal(barrier, **peer(*p)[1])

    def load(src, dst, sem):
        copy = pltpu.make_async_copy(src, dst, sem)
        copy.start()
        return copy

    span = filt.shape[1] // n_mid
    get_traces = load(traces_hbm, traces, load_sem.at[0])
    get_filter = [
        load(filter_hbm.at[:, pl.ds(i * span, span)], filt.at[:, pl.ds(i * span, span)], filt_sem.at[i])
        for i in range(n_mid)
    ]
    get_dft = []
    for i, dm in enumerate(far_first):
        m = lax.rem(mid + dm, n_mid)
        get_dft.append(load(dft_hbm.at[m], dft.at[m], dft_sem.at[i]))
    get_mid = load(mid_hbm, mid_ids, load_sem.at[1])
    get_off = load(off_hbm, off_ids, load_sem.at[2])
    get_level = load(level_hbm, level, load_sem.at[3])
    q = (freq * n_mid + mid) * n_off + off
    pairs = weights.shape[0]

    get_traces.wait()
    parts = []
    for i in range(n_mid):
        get_filter[i].wait()
        part = jnp.dot(traces[...], filt[:, i * span : (i + 1) * span], preferred_element_type=f32)
        parts.append(part.astype(bf16))
    folds = n_mid // 2
    stacked = jnp.concatenate([jnp.concatenate(parts[i * folds :][:folds], axis=1) for i in range(2)], axis=0)
    odd = lax.broadcasted_iota(jnp.int32, (1, group), 1) % 2 == 1
    get_mid.wait()
    get_off.wait()
    keys[off] = (off_ids[...] - off * half) * spacing + mid_ids[...]
    pl.semaphore_wait(barrier, total - 1)

    def id_copy(d):
        return send(keys.at[off], keys.at[off], id_send.at[d], id_recv.at[d], off=lax.rem(off + d, n_off))

    def block_copy(way, src, dst, p):
        there, device = peer(*p)
        return send(src.at[there], dst.at[index], send_sem.at[way, slot[p]], recv_sem.at[way, slot[p]], **device)

    for d in range(1, n_off):
        id_copy(d).start()
    for i, dm in enumerate(far_first):
        m = lax.rem(mid + dm, n_mid)
        get_dft[i].wait()
        if i == n_mid - 1:
            get_weights = load(table_hbm.at[pl.ds(q * pairs, pairs)], weights, load_sem.at[4])
            get_inv = load(inv_hbm, inv, load_sem.at[5])
        halves = jnp.dot(stacked, dft[m], preferred_element_type=f32)
        first, second = halves[: 2 * lines], halves[2 * lines :]
        spectra = (first + jnp.where(odd, -second, second)).astype(bf16)
        for o in range(n_off):
            for f in range(n_freq):
                at = (o * n_freq + f) * width
                block = jnp.concatenate([spectra[:lines, at : at + width], spectra[lines:, at : at + width]], axis=1)
                blocks[(o * n_mid + m) * n_freq + f] = block
        for p in peers:
            if p[0] == dm and p in others:
                block_copy(0, blocks, got, p).start()
    got[index] = blocks[index]

    get_level.wait()
    for k in range(count):
        own_level = level[(mid * n_off + off) * count + k]
        lev[k] = jnp.full((mids, NP), own_level * own_level, f32)
    for d in range(1, n_off):
        id_copy(d).wait_recv()

    def column_key(shape, dim, o):
        col = lax.broadcasted_iota(jnp.int32, shape, dim)
        j, u, h = col // NOFF, col // half % 2, col % half
        return (h * spacing + 2 * j + (u + o) % 2).astype(f32)

    for o in range(n_off):
        key = keys[o].astype(f32)
        n_src = total // n_off
        pieces = [key[:, s * 2 * lines + pk * lines :][:, :lines] for pk in range(2) for s in range(n_src)]
        key = jnp.concatenate(pieces, axis=1)
        cols = jnp.transpose(jnp.broadcast_to(key, (NOFF, per_half)))
        key_col[o] = cols
        col_of_lane = column_key((1, cells), 1, o)
        step = 64

        @pl.loop(0, per_half // step)
        def _(j):
            here = pl.multiple_of(j * step, step)
            own = key_col[o, pl.ds(here, step)]
            own = jnp.concatenate([own] * (cells // NOFF), axis=1)
            away = jnp.abs(own - col_of_lane)
            near[o, pl.ds(here, step)] = jnp.where(away == 0, 0.5, jnp.where(away == 1, 0.25, 0.0)).astype(bf16)

        @pl.loop(0, cells // step)
        def _(j):
            here = pl.multiple_of(j * step, step)
            col = lax.broadcasted_iota(jnp.int32, (step, NOFF), 0) + here
            c, u, h = col // NOFF, col // half % 2, col % half
            col = (h * spacing + 2 * c + (u + o) % 2).astype(f32)
            col = jnp.concatenate([col] * (per_half // NOFF), axis=1)
            same[o, pl.ds(here, step)] = jnp.where(col == key, 1.0, 0.0).astype(bf16)

    get_weights.wait()
    for p in others:
        block_copy(0, blocks, got, p).wait_recv()
    gathered = []
    n_src = total // n_off
    for o in range(n_off):
        rows = got[o * n_src : (o + 1) * n_src].reshape(n_src * lines, wide)
        rows = jnp.transpose(rows.astype(f32)).astype(bf16)
        rows = jnp.concatenate([rows[:width], rows[width:]], axis=1)
        gathered.append(jnp.dot(rows, near[o], preferred_element_type=f32))
    low = lax.broadcasted_iota(jnp.int32, (width, NOFF), 1) < half
    for j in range(mids // 2):
        a, b = (g[:, j * NOFF : (j + 1) * NOFF] for g in gathered)
        cube[pl.ds(2 * j, width, stride=mids), :] = jnp.where(low, a, b)
        cube[pl.ds(2 * j + 1, width, stride=mids), :] = pltpu.roll(jnp.where(low, b, a), half, 1)
    re, im = cube[...].reshape(2, count, mids, NOFF)
    first = jnp.concatenate([re, -im], axis=2)
    second = jnp.concatenate([im, re], axis=2)
    x = jnp.concatenate([first, second], axis=1).astype(bf16).reshape(pairs, 4 * mids, 2 * NOFF)
    both = lax.dot_general(x, weights[...], (((2,), (1,)), ((0,), (0,))), preferred_element_type=f32)
    keep = (lax.broadcasted_iota(jnp.int32, (mids, NP), 1) >= NP // 4).astype(f32)
    levels = lev[...].reshape(pairs, 2, mids, NP)
    kept = []
    for i in range(2):
        model_re = both[:, 2 * i * mids : (2 * i + 1) * mids, i * NP : (i + 1) * NP]
        model_im = both[:, (2 * i + 1) * mids : (2 * i + 2) * mids, i * NP : (i + 1) * NP]
        power = model_re * model_re + model_im * model_im
        factor = power / (power + levels[:, i]) * keep
        part = jnp.concatenate([model_re * factor, model_im * factor], axis=1)
        blank = jnp.zeros_like(part)
        kept.append(jnp.concatenate([blank] * i + [part] + [blank] * (1 - i), axis=2))
    kept = jnp.concatenate(kept, axis=1).astype(bf16)
    both = lax.dot_general(kept, weights[...], (((2,), (2,)), ((0,), (0,))), preferred_element_type=f32)
    both = both.reshape(count, 2 * mids, 2 * NOFF)
    mult_re = both[:, :mids, :NOFF] + both[:, mids:, NOFF:]
    mult_im = both[:, mids:, :NOFF] - both[:, :mids, NOFF:]
    cube[...] = jnp.concatenate([mult_re, mult_im], axis=0).reshape(width * mids, NOFF)
    mult = [[], []]
    for j in range(mids // 2):
        even = cube[pl.ds(2 * j, width, stride=mids), :]
        other = pltpu.roll(cube[pl.ds(2 * j + 1, width, stride=mids), :], half, 1)
        mult[0].append(jnp.where(low, even, other))
        mult[1].append(jnp.where(low, other, even))
    for o in range(n_off):
        routes[o] = jnp.concatenate(mult[o], axis=1).astype(bf16)
    for do in reversed(range(n_off)):
        o = lax.rem(off + do, n_off)
        routed = jnp.dot(routes[o], same[o], preferred_element_type=f32)
        routed = jnp.concatenate([routed[:, : per_half // 2], routed[:, per_half // 2 :]], axis=0)
        back[pl.ds(o * n_src, n_src)] = jnp.transpose(routed).astype(bf16).reshape(n_src, lines, wide)
        for p in others:
            if p[2] == do:
                block_copy(1, back, ret, p).start()
    ret[index] = back[index]

    get_inv.wait()
    low = lax.broadcasted_iota(jnp.int32, (lines, wide), 1) < width
    total_out = None
    for dm in reversed(far_first):
        m = lax.rem(mid + dm, n_mid)
        for p in others:
            if (p[0] + dm) % n_mid == 0:
                block_copy(1, back, ret, p).wait_recv()
        clean = []
        for o in range(n_off):
            for f in range(n_freq):
                d = (o * n_mid + m) * n_freq + f
                clean.append(blocks[d].astype(f32) - ret[d].astype(f32))
        top, bottom = [], []
        for i in range(0, len(clean), 2):
            top.append(jnp.where(low, clean[i], pltpu.roll(clean[i + 1], width, 1)))
            bottom.append(jnp.where(low, pltpu.roll(clean[i], width, 1), clean[i + 1]))
        clean = jnp.concatenate([jnp.concatenate(top, axis=1), jnp.concatenate(bottom, axis=1)], axis=0)
        clean = jnp.concatenate([clean, jnp.where(odd, -clean, clean)], axis=0).astype(bf16)
        sums = jnp.dot(clean, inv[m], preferred_element_type=f32)
        total_out = sums if total_out is None else total_out + sums
    n_time = inv.shape[2]
    out[:, :n_time] = total_out[: 2 * lines].astype(bf16)
    out[:, n_time:] = total_out[2 * lines :].astype(bf16)
    for way, src, dst in ((0, blocks, got), (1, back, ret)):
        for p in others:
            block_copy(way, src, dst, p).wait_send()
    for d in range(1, n_off):
        id_copy(d).wait_send()


def fused(traces, time_filter, midpoint_of, offset_of, level, dft, inv, table, sizes):
    n_off, n_mid, n_freq = sizes
    total = n_off * n_mid * n_freq
    count = level.shape[0] // (n_mid * n_off)
    width = 2 * count
    lines = traces.shape[0] // 2
    per_half = midpoint_of.shape[1]
    mids = n_off * per_half // NOFF
    cells = per_half
    dma = pltpu.SemaphoreType.DMA
    f32, bf16, i32 = jnp.float32, jnp.bfloat16, jnp.int32
    shape = (total, lines, 2 * width)
    hbm = pl.BlockSpec(memory_space=pltpu.HBM)
    operands = (traces, time_filter, midpoint_of, offset_of, level, dft, inv, table)
    return pl.pallas_call(
        functools.partial(fused_kernel, sizes),
        out_shape=jax.ShapeDtypeStruct(traces.shape, traces.dtype),
        in_specs=[hbm] * 8,
        out_specs=VMEM,
        scratch_shapes=[
            pltpu.VMEM(traces.shape, bf16),
            pltpu.VMEM(time_filter.shape, bf16),
            pltpu.VMEM(midpoint_of.shape, i32),
            pltpu.VMEM(offset_of.shape, i32),
            pltpu.SMEM(level.shape, f32),
            pltpu.VMEM(dft.shape, bf16),
            pltpu.VMEM(inv.shape, bf16),
            pltpu.VMEM((count // 2,) + table.shape[1:], bf16),
            pltpu.VMEM((n_off, 1, per_half), i32),
            pltpu.VMEM((n_off, per_half, NOFF), f32),
            pltpu.VMEM((n_off, per_half, cells), bf16),
            pltpu.VMEM((n_off, cells, per_half), bf16),
            pltpu.VMEM(shape, bf16),
            pltpu.VMEM(shape, bf16),
            pltpu.VMEM(shape, bf16),
            pltpu.VMEM(shape, bf16),
            pltpu.VMEM((n_off, width, cells), bf16),
            pltpu.VMEM((width * mids, NOFF), f32),
            pltpu.VMEM((count, mids, NP), f32),
            dma((6,)),
            dma((n_mid,)),
            dma((n_mid,)),
            dma((2, total)),
            dma((2, total)),
            dma((n_off,)),
            dma((n_off,)),
        ],
        compiler_params=pltpu.CompilerParams(
            collective_id=2, has_side_effects=True, vmem_limit_bytes=32 * 1024 * 1024
        ),
    )(*(pltpu.with_memory_space_constraint(x, pltpu.HBM) for x in operands))


def small(n_traces, n_off, width):
    return n_traces <= 4096 and n_off == 2 and width == 64


def on_device(dft, inv, weights, traces, time_filter, midpoint_of, offset_of, shrink_level):
    n_mid = lax.axis_size("mid")
    n_freq = lax.axis_size("freq")
    n_off = lax.axis_size("off")
    sizes = (n_off, n_mid, n_freq)
    total = n_off * n_mid * n_freq
    me_mid = lax.axis_index("mid")
    me_off = lax.axis_index("off")
    tr_dev = traces.shape[1]
    count = shrink_level.shape[0] // (n_mid * n_off)
    width = 2 * count
    pack = max(1, min(tr_dev, 128 // width))
    n_traces = total * tr_dev
    n_mids = n_traces // NOFF
    f32, bf16 = jnp.float32, jnp.bfloat16

    if small(n_traces, n_off, width):
        return fused(traces[0], time_filter, midpoint_of, offset_of, shrink_level, dft, inv, weights, sizes)[None]
    own_ids = midpoint_of * NOFF + offset_of
    filtered = jnp.dot(traces[0], time_filter, preferred_element_type=f32).astype(bf16)
    spectra = jnp.dot(filtered, dft, preferred_element_type=f32).astype(bf16)
    blocks = spectra.reshape(pack, tr_dev // pack, total, width)
    blocks = jnp.transpose(blocks, (2, 1, 0, 3)).reshape(total, tr_dev // pack, pack * width)
    own_levels = lax.dynamic_slice_in_dim(shrink_level, (me_mid * n_off + me_off) * count, count)
    level = jnp.broadcast_to(own_levels[:, None, None], (count, 1, NP))
    rows, ids = swap(blocks, sizes, 0, own_ids)
    rows = rows.reshape(total, tr_dev // pack, pack, width)
    rows = jnp.transpose(rows, (0, 2, 1, 3)).reshape(n_traces, width)
    cell_of = ids.reshape(n_traces)
    gather = jnp.zeros((n_traces, width), bf16).at[cell_of].set(rows)
    edged = jnp.pad(gather.reshape(n_mids, NOFF, 2, count).astype(f32), ((1, 1), (0, 0), (0, 0), (0, 0)))
    smooth = ((edged[:-2] + 2.0 * edged[1:-1] + edged[2:]) * 0.25).astype(bf16)
    smooth = jnp.transpose(smooth, (2, 3, 0, 1))
    mult = radon(smooth, level, weights, n_mid, n_off).reshape(width, n_traces)
    back = jnp.transpose(mult)[cell_of].reshape(total, pack, tr_dev // pack, width)
    back = jnp.transpose(back, (0, 2, 1, 3)).reshape(total, tr_dev // pack, pack * width)
    (returned,) = swap(back, sizes, 1)
    returned = returned.reshape(total, tr_dev // pack, pack, width)
    own_mult = jnp.transpose(returned, (2, 1, 0, 3)).reshape(tr_dev, total * width)
    clean = (spectra.astype(f32) - own_mult.astype(f32)).astype(bf16)
    sums = lax.dot_general(clean, dft, (((1,), (1,)), ((), ())), preferred_element_type=f32)
    return (2.0 * sums).astype(bf16)[None]


def solution(mesh):
    n_freq, n_mid, n_off = (mesh.shape[name] for name in ("freq", "mid", "off"))

    def run(traces, time_filter, midpoint_of, offset_of, shrink_level):
        n_freqs = shrink_level.shape[0]
        n_time = traces.shape[2]
        pieces = n_freq * n_mid * n_off
        count = n_freqs // pieces
        dft = dft_table(n_time, pieces, count).reshape(n_time, n_freq, n_mid, n_off, -1)
        weights = radon_table(n_freqs)
        part_traces = traces.shape[0] * traces.shape[1] // mesh.shape["group"]
        if small(part_traces, n_off, 2 * count):
            dft = np.ascontiguousarray(dft[: n_time // 2].transpose(2, 0, 3, 1, 4)).reshape(n_mid, n_time // 2, -1)
            inv = np.ascontiguousarray(dft.transpose(0, 2, 1)) * np.asarray(2, dft.dtype)
            weights = weights.reshape(n_freqs // 2, 2, 2 * NOFF, NP).transpose(0, 2, 1, 3)
            weights = np.ascontiguousarray(weights).reshape(n_freqs // 2, 2 * NOFF, 2 * NP)
        else:
            dft = np.ascontiguousarray(dft.transpose(0, 3, 2, 1, 4)).reshape(n_time, 2 * n_freqs)
            inv = np.zeros((1,), dft.dtype)
        return jax.shard_map(
            on_device,
            mesh=mesh,
            in_specs=(
                P(),
                P(),
                P(),
                P("off", ("group", "mid", "freq"), None),
                P(),
                P("off", "group"),
                P("off", "group"),
                P("freq"),
            ),
            out_specs=P("off", ("group", "mid", "freq"), None),
            check_vma=False,
        )(jnp.asarray(dft), jnp.asarray(inv), jnp.asarray(weights), traces, time_filter, midpoint_of, offset_of, shrink_level)

    return run
```

```python
import functools
import math

import jax
import jax.numpy as jnp
import numpy as np
from jax import lax
from jax.experimental import pallas as pl
from jax.experimental.pallas import tpu as pltpu
from jax.sharding import PartitionSpec as P

NOFF = 128
NP = 128
radon_period = 4096
VMEM = pl.BlockSpec(memory_space=pltpu.VMEM)
ANY = pl.BlockSpec(memory_space=pl.ANY)


def dft_table(n_time, n_bands, band_size):
    sample = np.arange(n_time, dtype=np.int64)[:, None]
    freq_index = np.arange(n_bands * band_size, dtype=np.int64)[None, :]
    angle = 2.0 * np.pi * (sample * freq_index % n_time) / n_time
    scale_f = 1.0 / math.sqrt(n_time)
    cosine = (np.cos(angle) * scale_f).reshape(n_time, n_bands, band_size)
    sine = (-np.sin(angle) * scale_f).reshape(n_time, n_bands, band_size)
    table = np.stack([cosine, sine], axis=2).reshape(n_time, n_bands * 2 * band_size)
    return table.astype(np.float32).astype(jnp.bfloat16)


def radon_table(n_freqs):
    freq_index = np.arange(n_freqs, dtype=np.int64)[:, None, None]
    offset_index = np.arange(NOFF, dtype=np.int64)[None, :, None]
    slowness = np.arange(NP, dtype=np.int64)[None, None, :]
    turns = freq_index * slowness % radon_period * (offset_index * offset_index % radon_period) % radon_period
    circle = 2.0 * np.pi * np.arange(radon_period) / radon_period
    scale_r = 1.0 / math.sqrt(NOFF)
    cosine = (np.cos(circle) * scale_r).astype(np.float32).astype(jnp.bfloat16)[turns]
    sine = (np.sin(circle) * scale_r).astype(np.float32).astype(jnp.bfloat16)[turns]
    return np.stack([cosine, sine], axis=1).reshape(n_freqs, 2 * NOFF, NP)


def signal(barrier, **device):
    pl.semaphore_signal(barrier, inc=1, device_id=device, device_id_type=pl.DeviceIdType.MESH)


def send(src, dst, send_sem, recv_sem, **device):
    return pltpu.make_async_remote_copy(
        src_ref=src,
        dst_ref=dst,
        send_sem=send_sem,
        recv_sem=recv_sem,
        device_id=device,
        device_id_type=pl.DeviceIdType.MESH,
    )


def place(sizes):
    names = ("off", "mid", "freq")
    here = [lax.axis_index(name) for name in names]
    index = (here[0] * sizes[1] + here[1]) * sizes[2] + here[2]
    total = sizes[0] * sizes[1] * sizes[2]

    def ahead(i):
        there = (index + i) % total
        return there, dict(off=there // (sizes[1] * sizes[2]), mid=there // sizes[2] % sizes[1], freq=there % sizes[2])

    return index, total, ahead


def swap_kernel(sizes, with_ids, *refs):
    if with_ids:
        blocks, ids, got, got_ids, own_sem, send_sem, recv_sem, id_own, id_send, id_recv = refs
    else:
        blocks, got, own_sem, send_sem, recv_sem = refs
    index, total, ahead = place(sizes)
    n_off = sizes[0]
    barrier = pltpu.get_barrier_semaphore()

    @pl.loop(1, total)
    def _(i):
        signal(barrier, **ahead(i)[1])

    own = pltpu.make_async_copy(blocks.at[index], got.at[index], own_sem)
    own.start()
    pl.semaphore_wait(barrier, total - 1)

    def block_copy(i):
        there, device = ahead(i)
        return send(blocks.at[there], got.at[index], send_sem.at[i], recv_sem.at[i], **device)

    def id_copy(d):
        off = lax.axis_index("off")
        return send(ids, got_ids.at[off], id_send.at[d], id_recv.at[d], off=(off + d) % n_off)

    if with_ids:
        own_ids = pltpu.make_async_copy(ids, got_ids.at[lax.axis_index("off")], id_own)
        own_ids.start()
        for d in range(1, n_off):
            id_copy(d).start()

    @pl.loop(1, total)
    def _(i):
        block_copy(i).start()

    own.wait()
    if with_ids:
        own_ids.wait()
        for d in range(1, n_off):
            id_copy(d).wait()

    @pl.loop(1, total)
    def _(i):
        block_copy(i).wait()


def swap(blocks, sizes, collective_id, ids=None):
    total, n_off = blocks.shape[0], sizes[0]
    dma = pltpu.SemaphoreType.DMA
    shapes = [jax.ShapeDtypeStruct(blocks.shape, blocks.dtype)]
    scratch = [dma, dma((total,)), dma((total,))]
    operands = [blocks]
    if ids is not None:
        shapes.append(jax.ShapeDtypeStruct((n_off,) + ids.shape, ids.dtype))
        scratch += [dma, dma((n_off,)), dma((n_off,))]
        operands.append(ids)
    return pl.pallas_call(
        functools.partial(swap_kernel, sizes, ids is not None),
        out_shape=shapes,
        in_specs=[VMEM] * len(operands),
        out_specs=[VMEM] * len(shapes),
        scratch_shapes=scratch,
        compiler_params=pltpu.CompilerParams(collective_id=collective_id, has_side_effects=True),
    )(*operands)


def radon_kernel(n_mid, n_off, smooth, level, table, out, weights, sem):
    count, mids = smooth.shape[1:3]
    q = (lax.axis_index("freq") * n_mid + lax.axis_index("mid")) * n_off + lax.axis_index("off")
    fetch = pltpu.make_async_copy(table.at[pl.ds(q * count, count)], weights, sem)
    fetch.start()
    re = smooth[0].astype(jnp.float32)
    im = smooth[1].astype(jnp.float32)
    first = jnp.concatenate([re, -im], axis=2)
    second = jnp.concatenate([im, re], axis=2)
    x = jnp.concatenate([first, second], axis=1).astype(jnp.bfloat16)
    fetch.wait()
    model = lax.dot_general(x, weights[...], (((2,), (1,)), ((0,), (0,))), preferred_element_type=jnp.float32)
    model_re, model_im = model[:, :mids], model[:, mids:]
    power = model_re * model_re + model_im * model_im
    keep = (lax.broadcasted_iota(jnp.int32, power.shape, 2) >= NP // 4).astype(jnp.float32)
    lev = level[...]
    factor = power / (power + lev * lev) * keep
    kept = jnp.concatenate([model_re * factor, model_im * factor], axis=1).astype(jnp.bfloat16)
    both = lax.dot_general(kept, weights[...], (((2,), (2,)), ((0,), (0,))), preferred_element_type=jnp.float32)
    out[0] = (both[:, :mids, :NOFF] + both[:, mids:, NOFF:]).astype(jnp.bfloat16)
    out[1] = (both[:, mids:, :NOFF] - both[:, :mids, NOFF:]).astype(jnp.bfloat16)


def radon(smooth, level, table, n_mid, n_off):
    count = smooth.shape[1]
    return pl.pallas_call(
        functools.partial(radon_kernel, n_mid, n_off),
        out_shape=jax.ShapeDtypeStruct(smooth.shape, jnp.bfloat16),
        in_specs=[VMEM, VMEM, ANY],
        out_specs=VMEM,
        scratch_shapes=[pltpu.VMEM((count, 2 * NOFF, NP), jnp.bfloat16), pltpu.SemaphoreType.DMA],
        compiler_params=pltpu.CompilerParams(vmem_limit_bytes=24 * 1024 * 1024),
    )(smooth, level, table)


def fused_kernel(sizes, traces_hbm, filter_hbm, mid_hbm, off_hbm, level_hbm, dft_hbm, inv_hbm, table_hbm, out, traces, filt, mid_ids, off_ids, level, dft, inv, weights, keys, key_col, near, same, blocks, got, back, ret, routes, cube, lev, load_sem, filt_sem, dft_sem, send_sem, recv_sem, id_send, id_recv):
    n_off, n_mid, n_freq = sizes
    total = n_off * n_mid * n_freq
    off, mid, freq = (lax.axis_index(name) for name in ("off", "mid", "freq"))
    f32, bf16 = jnp.float32, jnp.bfloat16
    lines, wide = blocks.shape[1:]
    width = wide // 2
    count = width // 2
    half = NOFF // n_off
    mids = lev.shape[1]
    cells = mids * half
    per_half = keys.shape[2]
    spacing = 2 * mids
    group = n_off * n_freq * width

    def peer(dm, df, do):
        m, f, o = lax.rem(mid + dm, n_mid), lax.rem(freq + df, n_freq), lax.rem(off + do, n_off)
        return (o * n_mid + m) * n_freq + f, dict(off=o, mid=m, freq=f)

    index = (off * n_mid + mid) * n_freq + freq
    far_first = sorted(range(n_mid), key=lambda dm: (dm == 0, abs(dm - n_mid // 2)))
    peers = [(dm, df, do) for do in reversed(range(n_off)) for df in reversed(range(n_freq)) for dm in far_first]
    slot = {p: i for i, p in enumerate(peers)}
    others = [p for p in peers if p != (0, 0, 0)]
    barrier = pltpu.get_barrier_semaphore()
    for p in others:
        signal(barrier, **peer(*p)[1])

    def load(src, dst, sem):
        copy = pltpu.make_async_copy(src, dst, sem)
        copy.start()
        return copy

    span = filt.shape[1] // n_mid
    get_traces = load(traces_hbm, traces, load_sem.at[0])
    get_filter = [
        load(filter_hbm.at[:, pl.ds(i * span, span)], filt.at[:, pl.ds(i * span, span)], filt_sem.at[i])
        for i in range(n_mid)
    ]
    get_mid = load(mid_hbm, mid_ids, load_sem.at[1])
    get_off = load(off_hbm, off_ids, load_sem.at[2])
    get_level = load(level_hbm, level, load_sem.at[3])
    q = (freq * n_mid + mid) * n_off + off
    pairs = weights.shape[0]

    get_traces.wait()
    parts = []
    for i in range(n_mid):
        get_filter[i].wait()
        if i == 0:
            get_dft = [load(dft_hbm.at[m], dft.at[m], dft_sem.at[m]) for m in range(n_mid)]
        part = jnp.dot(traces[...], filt[:, i * span : (i + 1) * span], preferred_element_type=f32)
        parts.append(part.astype(bf16))
    folds = n_mid // 2
    stacked = jnp.concatenate([jnp.concatenate(parts[i * folds :][:folds], axis=1) for i in range(2)], axis=0)
    odd = lax.broadcasted_iota(jnp.int32, (1, group), 1) % 2 == 1
    def id_copy(d):
        return send(keys.at[off], keys.at[off], id_send.at[d], id_recv.at[d], off=lax.rem(off + d, n_off))

    def block_copy(way, src, dst, p):
        there, device = peer(*p)
        return send(src.at[there], dst.at[index], send_sem.at[way, slot[p]], recv_sem.at[way, slot[p]], **device)

    for get in get_dft:
        get.wait()
    get_weights = load(table_hbm.at[pl.ds(q * pairs, pairs)], weights, load_sem.at[4])
    get_inv = load(inv_hbm, inv, load_sem.at[5])
    low = lax.broadcasted_iota(jnp.int32, (lines, wide), 1) < width
    for m in range(n_mid):
        halves = jnp.dot(stacked, dft[m], preferred_element_type=f32)
        first, second = halves[: 2 * lines], halves[2 * lines :]
        spectra = first + jnp.where(odd, -second, second)
        for i in range(0, n_off * n_freq, 2):
            top, bottom = (spectra[pk * lines :, i * width :][:lines, :wide] for pk in range(2))
            pair = jnp.where(low, top, pltpu.roll(bottom, width, 1)), jnp.where(low, pltpu.roll(top, width, 1), bottom)
            for at in range(2):
                o, f = (i + at) // n_freq, (i + at) % n_freq
                blocks[(o * n_mid + m) * n_freq + f] = pair[at].astype(bf16)
    get_mid.wait()
    get_off.wait()
    keys[off] = (off_ids[...] - off * half) * spacing + mid_ids[...]
    pl.semaphore_wait(barrier, total - 1)
    for d in range(1, n_off):
        id_copy(d).start()
    for p in others:
        block_copy(0, blocks, got, p).start()
    got[index] = blocks[index]

    get_level.wait()
    for k in range(count):
        own_level = level[(mid * n_off + off) * count + k]
        lev[k] = jnp.full((mids, NP), own_level * own_level, f32)
    for d in range(1, n_off):
        id_copy(d).wait_recv()

    def column_key(shape, dim, o):
        col = lax.broadcasted_iota(jnp.int32, shape, dim)
        j, u, h = col // NOFF, col // half % 2, col % half
        return (h * spacing + 2 * j + (u + o) % 2).astype(f32)

    for o in range(n_off):
        key = keys[o].astype(f32)
        n_src = total // n_off
        pieces = [key[:, s * 2 * lines + pk * lines :][:, :lines] for pk in range(2) for s in range(n_src)]
        key = jnp.concatenate(pieces, axis=1)
        cols = jnp.transpose(jnp.broadcast_to(key, (NOFF, per_half)))
        key_col[o] = cols
        col_of_lane = column_key((1, cells), 1, o)
        step = 64

        @pl.loop(0, per_half // step)
        def _(j):
            here = pl.multiple_of(j * step, step)
            own = key_col[o, pl.ds(here, step)]
            own = jnp.concatenate([own] * (cells // NOFF), axis=1)
            away = jnp.abs(own - col_of_lane)
            near[o, pl.ds(here, step)] = jnp.where(away == 0, 0.5, jnp.where(away == 1, 0.25, 0.0)).astype(bf16)

        @pl.loop(0, cells // step)
        def _(j):
            here = pl.multiple_of(j * step, step)
            col = lax.broadcasted_iota(jnp.int32, (step, NOFF), 0) + here
            c, u, h = col // NOFF, col // half % 2, col % half
            col = (h * spacing + 2 * c + (u + o) % 2).astype(f32)
            col = jnp.concatenate([col] * (per_half // NOFF), axis=1)
            same[o, pl.ds(here, step)] = jnp.where(col == key, 1.0, 0.0).astype(bf16)

    get_weights.wait()
    for p in others:
        block_copy(0, blocks, got, p).wait_recv()
    gathered = []
    n_src = total // n_off
    for o in range(n_off):
        rows = got[o * n_src : (o + 1) * n_src].reshape(n_src * lines, wide)
        rows = jnp.transpose(rows.astype(f32)).astype(bf16)
        rows = jnp.concatenate([rows[:width], rows[width:]], axis=1)
        gathered.append(jnp.dot(rows, near[o], preferred_element_type=f32))
    low = lax.broadcasted_iota(jnp.int32, (width, NOFF), 1) < half
    for j in range(mids // 2):
        a, b = (g[:, j * NOFF : (j + 1) * NOFF] for g in gathered)
        cube[pl.ds(2 * j, width, stride=mids), :] = jnp.where(low, a, b)
        cube[pl.ds(2 * j + 1, width, stride=mids), :] = pltpu.roll(jnp.where(low, b, a), half, 1)
    re, im = cube[...].reshape(2, count, mids, NOFF)
    first = jnp.concatenate([re, -im], axis=2)
    second = jnp.concatenate([im, re], axis=2)
    x = jnp.concatenate([first, second], axis=1).astype(bf16).reshape(pairs, 4 * mids, 2 * NOFF)
    both = lax.dot_general(x, weights[...], (((2,), (1,)), ((0,), (0,))), preferred_element_type=f32)
    keep = (lax.broadcasted_iota(jnp.int32, (mids, NP), 1) >= NP // 4).astype(f32)
    levels = lev[...].reshape(pairs, 2, mids, NP)
    kept = []
    for i in range(2):
        model_re = both[:, 2 * i * mids : (2 * i + 1) * mids, i * NP : (i + 1) * NP]
        model_im = both[:, (2 * i + 1) * mids : (2 * i + 2) * mids, i * NP : (i + 1) * NP]
        power = model_re * model_re + model_im * model_im
        factor = power / (power + levels[:, i]) * keep
        part = jnp.concatenate([model_re * factor, model_im * factor], axis=1)
        blank = jnp.zeros_like(part)
        kept.append(jnp.concatenate([blank] * i + [part] + [blank] * (1 - i), axis=2))
    kept = jnp.concatenate(kept, axis=1).astype(bf16)
    both = lax.dot_general(kept, weights[...], (((2,), (2,)), ((0,), (0,))), preferred_element_type=f32)
    both = both.reshape(count, 2 * mids, 2 * NOFF)
    mult_re = both[:, :mids, :NOFF] + both[:, mids:, NOFF:]
    mult_im = both[:, mids:, :NOFF] - both[:, :mids, NOFF:]
    cube[...] = jnp.concatenate([mult_re, mult_im], axis=0).reshape(width * mids, NOFF)
    mult = [[], []]
    for j in range(mids // 2):
        even = cube[pl.ds(2 * j, width, stride=mids), :]
        other = pltpu.roll(cube[pl.ds(2 * j + 1, width, stride=mids), :], half, 1)
        mult[0].append(jnp.where(low, even, other))
        mult[1].append(jnp.where(low, other, even))
    for o in range(n_off):
        routes[o] = jnp.concatenate(mult[o], axis=1).astype(bf16)
    for do in reversed(range(n_off)):
        o = lax.rem(off + do, n_off)
        routed = jnp.dot(routes[o], same[o], preferred_element_type=f32)
        routed = jnp.concatenate([routed[:, : per_half // 2], routed[:, per_half // 2 :]], axis=0)
        back[pl.ds(o * n_src, n_src)] = jnp.transpose(routed).astype(bf16).reshape(n_src, lines, wide)
        for p in others:
            if p[2] == do:
                block_copy(1, back, ret, p).start()
    ret[index] = back[index]

    get_inv.wait()
    low = lax.broadcasted_iota(jnp.int32, (lines, wide), 1) < width
    total_out = None
    for dm in reversed(far_first):
        m = lax.rem(mid + dm, n_mid)
        for p in others:
            if (p[0] + dm) % n_mid == 0:
                block_copy(1, back, ret, p).wait_recv()
        clean = []
        for o in range(n_off):
            for f in range(n_freq):
                d = (o * n_mid + m) * n_freq + f
                clean.append(blocks[d].astype(f32) - ret[d].astype(f32))
        top, bottom = [], []
        for i in range(0, len(clean), 2):
            top.append(jnp.where(low, clean[i], pltpu.roll(clean[i + 1], width, 1)))
            bottom.append(jnp.where(low, pltpu.roll(clean[i], width, 1), clean[i + 1]))
        clean = jnp.concatenate([jnp.concatenate(top, axis=1), jnp.concatenate(bottom, axis=1)], axis=0)
        clean = jnp.concatenate([clean, jnp.where(odd, -clean, clean)], axis=0).astype(bf16)
        sums = jnp.dot(clean, inv[m], preferred_element_type=f32)
        total_out = sums if total_out is None else total_out + sums
    n_time = inv.shape[2]
    out[:, :n_time] = total_out[: 2 * lines].astype(bf16)
    out[:, n_time:] = total_out[2 * lines :].astype(bf16)
    for way, src, dst in ((0, blocks, got), (1, back, ret)):
        for p in others:
            block_copy(way, src, dst, p).wait_send()
    for d in range(1, n_off):
        id_copy(d).wait_send()


def fused(traces, time_filter, midpoint_of, offset_of, level, dft, inv, table, sizes):
    n_off, n_mid, n_freq = sizes
    total = n_off * n_mid * n_freq
    count = level.shape[0] // (n_mid * n_off)
    width = 2 * count
    lines = traces.shape[0] // 2
    per_half = midpoint_of.shape[1]
    mids = n_off * per_half // NOFF
    cells = per_half
    dma = pltpu.SemaphoreType.DMA
    f32, bf16, i32 = jnp.float32, jnp.bfloat16, jnp.int32
    shape = (total, lines, 2 * width)
    hbm = pl.BlockSpec(memory_space=pltpu.HBM)
    operands = (traces, time_filter, midpoint_of, offset_of, level, dft, inv, table)
    return pl.pallas_call(
        functools.partial(fused_kernel, sizes),
        out_shape=jax.ShapeDtypeStruct(traces.shape, traces.dtype),
        in_specs=[hbm] * 8,
        out_specs=VMEM,
        scratch_shapes=[
            pltpu.VMEM(traces.shape, bf16),
            pltpu.VMEM(time_filter.shape, bf16),
            pltpu.VMEM(midpoint_of.shape, i32),
            pltpu.VMEM(offset_of.shape, i32),
            pltpu.SMEM(level.shape, f32),
            pltpu.VMEM(dft.shape, bf16),
            pltpu.VMEM(inv.shape, bf16),
            pltpu.VMEM((count // 2,) + table.shape[1:], bf16),
            pltpu.VMEM((n_off, 1, per_half), i32),
            pltpu.VMEM((n_off, per_half, NOFF), f32),
            pltpu.VMEM((n_off, per_half, cells), bf16),
            pltpu.VMEM((n_off, cells, per_half), bf16),
            pltpu.VMEM(shape, bf16),
            pltpu.VMEM(shape, bf16),
            pltpu.VMEM(shape, bf16),
            pltpu.VMEM(shape, bf16),
            pltpu.VMEM((n_off, width, cells), bf16),
            pltpu.VMEM((width * mids, NOFF), f32),
            pltpu.VMEM((count, mids, NP), f32),
            dma((6,)),
            dma((n_mid,)),
            dma((n_mid,)),
            dma((2, total)),
            dma((2, total)),
            dma((n_off,)),
            dma((n_off,)),
        ],
        compiler_params=pltpu.CompilerParams(
            collective_id=2, has_side_effects=True, vmem_limit_bytes=32 * 1024 * 1024
        ),
    )(*(pltpu.with_memory_space_constraint(x, pltpu.HBM) for x in operands))


def small(n_traces, n_off, width):
    return n_traces <= 4096 and n_off == 2 and width == 64


def on_device(dft, inv, weights, traces, time_filter, midpoint_of, offset_of, shrink_level):
    n_mid = lax.axis_size("mid")
    n_freq = lax.axis_size("freq")
    n_off = lax.axis_size("off")
    sizes = (n_off, n_mid, n_freq)
    total = n_off * n_mid * n_freq
    me_mid = lax.axis_index("mid")
    me_off = lax.axis_index("off")
    tr_dev = traces.shape[1]
    count = shrink_level.shape[0] // (n_mid * n_off)
    width = 2 * count
    pack = max(1, min(tr_dev, 128 // width))
    n_traces = total * tr_dev
    n_mids = n_traces // NOFF
    f32, bf16 = jnp.float32, jnp.bfloat16

    if small(n_traces, n_off, width):
        return fused(traces[0], time_filter, midpoint_of, offset_of, shrink_level, dft, inv, weights, sizes)[None]
    own_ids = midpoint_of * NOFF + offset_of
    filtered = jnp.dot(traces[0], time_filter, preferred_element_type=f32).astype(bf16)
    spectra = jnp.dot(filtered, dft, preferred_element_type=f32).astype(bf16)
    blocks = spectra.reshape(pack, tr_dev // pack, total, width)
    blocks = jnp.transpose(blocks, (2, 1, 0, 3)).reshape(total, tr_dev // pack, pack * width)
    own_levels = lax.dynamic_slice_in_dim(shrink_level, (me_mid * n_off + me_off) * count, count)
    level = jnp.broadcast_to(own_levels[:, None, None], (count, 1, NP))
    rows, ids = swap(blocks, sizes, 0, own_ids)
    rows = rows.reshape(total, tr_dev // pack, pack, width)
    rows = jnp.transpose(rows, (0, 2, 1, 3)).reshape(n_traces, width)
    cell_of = ids.reshape(n_traces)
    gather = jnp.zeros((n_traces, width), bf16).at[cell_of].set(rows)
    edged = jnp.pad(gather.reshape(n_mids, NOFF, 2, count).astype(f32), ((1, 1), (0, 0), (0, 0), (0, 0)))
    smooth = ((edged[:-2] + 2.0 * edged[1:-1] + edged[2:]) * 0.25).astype(bf16)
    smooth = jnp.transpose(smooth, (2, 3, 0, 1))
    mult = radon(smooth, level, weights, n_mid, n_off).reshape(width, n_traces)
    back = jnp.transpose(mult)[cell_of].reshape(total, pack, tr_dev // pack, width)
    back = jnp.transpose(back, (0, 2, 1, 3)).reshape(total, tr_dev // pack, pack * width)
    (returned,) = swap(back, sizes, 1)
    returned = returned.reshape(total, tr_dev // pack, pack, width)
    own_mult = jnp.transpose(returned, (2, 1, 0, 3)).reshape(tr_dev, total * width)
    clean = (spectra.astype(f32) - own_mult.astype(f32)).astype(bf16)
    sums = lax.dot_general(clean, dft, (((1,), (1,)), ((), ())), preferred_element_type=f32)
    return (2.0 * sums).astype(bf16)[None]


def solution(mesh):
    n_freq, n_mid, n_off = (mesh.shape[name] for name in ("freq", "mid", "off"))

    def run(traces, time_filter, midpoint_of, offset_of, shrink_level):
        n_freqs = shrink_level.shape[0]
        n_time = traces.shape[2]
        pieces = n_freq * n_mid * n_off
        count = n_freqs // pieces
        dft = dft_table(n_time, pieces, count).reshape(n_time, n_freq, n_mid, n_off, -1)
        weights = radon_table(n_freqs)
        part_traces = traces.shape[0] * traces.shape[1] // mesh.shape["group"]
        if small(part_traces, n_off, 2 * count):
            dft = np.ascontiguousarray(dft[: n_time // 2].transpose(2, 0, 3, 1, 4)).reshape(n_mid, n_time // 2, -1)
            inv = np.ascontiguousarray(dft.transpose(0, 2, 1)) * np.asarray(2, dft.dtype)
            weights = weights.reshape(n_freqs // 2, 2, 2 * NOFF, NP).transpose(0, 2, 1, 3)
            weights = np.ascontiguousarray(weights).reshape(n_freqs // 2, 2 * NOFF, 2 * NP)
        else:
            dft = np.ascontiguousarray(dft.transpose(0, 3, 2, 1, 4)).reshape(n_time, 2 * n_freqs)
            inv = np.zeros((1,), dft.dtype)
        return jax.shard_map(
            on_device,
            mesh=mesh,
            in_specs=(
                P(),
                P(),
                P(),
                P("off", ("group", "mid", "freq"), None),
                P(),
                P("off", "group"),
                P("off", "group"),
                P("freq"),
            ),
            out_specs=P("off", ("group", "mid", "freq"), None),
            check_vma=False,
        )(jnp.asarray(dft), jnp.asarray(inv), jnp.asarray(weights), traces, time_filter, midpoint_of, offset_of, shrink_level)

    return run
```

```python
import functools
import math

import jax
import jax.numpy as jnp
import numpy as np
from jax import lax
from jax.experimental import pallas as pl
from jax.experimental.pallas import tpu as pltpu
from jax.sharding import PartitionSpec as P

NOFF = 128
NP = 128
radon_period = 4096
VMEM = pl.BlockSpec(memory_space=pltpu.VMEM)
ANY = pl.BlockSpec(memory_space=pl.ANY)


def dft_table(n_time, n_bands, band_size):
    sample = np.arange(n_time, dtype=np.int64)[:, None]
    freq_index = np.arange(n_bands * band_size, dtype=np.int64)[None, :]
    angle = 2.0 * np.pi * (sample * freq_index % n_time) / n_time
    scale_f = 1.0 / math.sqrt(n_time)
    cosine = (np.cos(angle) * scale_f).reshape(n_time, n_bands, band_size)
    sine = (-np.sin(angle) * scale_f).reshape(n_time, n_bands, band_size)
    table = np.stack([cosine, sine], axis=2).reshape(n_time, n_bands * 2 * band_size)
    return table.astype(np.float32).astype(jnp.bfloat16)


def radon_table(n_freqs):
    freq_index = np.arange(n_freqs, dtype=np.int64)[:, None, None]
    offset_index = np.arange(NOFF, dtype=np.int64)[None, :, None]
    slowness = np.arange(NP, dtype=np.int64)[None, None, :]
    turns = freq_index * slowness % radon_period * (offset_index * offset_index % radon_period) % radon_period
    circle = 2.0 * np.pi * np.arange(radon_period) / radon_period
    scale_r = 1.0 / math.sqrt(NOFF)
    cosine = (np.cos(circle) * scale_r).astype(np.float32).astype(jnp.bfloat16)[turns]
    sine = (np.sin(circle) * scale_r).astype(np.float32).astype(jnp.bfloat16)[turns]
    return np.stack([cosine, sine], axis=1).reshape(n_freqs, 2 * NOFF, NP)


def signal(barrier, **device):
    pl.semaphore_signal(barrier, inc=1, device_id=device, device_id_type=pl.DeviceIdType.MESH)


def send(src, dst, send_sem, recv_sem, **device):
    return pltpu.make_async_remote_copy(
        src_ref=src,
        dst_ref=dst,
        send_sem=send_sem,
        recv_sem=recv_sem,
        device_id=device,
        device_id_type=pl.DeviceIdType.MESH,
    )


def place(sizes):
    names = ("off", "mid", "freq")
    here = [lax.axis_index(name) for name in names]
    index = (here[0] * sizes[1] + here[1]) * sizes[2] + here[2]
    total = sizes[0] * sizes[1] * sizes[2]

    def ahead(i):
        there = (index + i) % total
        return there, dict(off=there // (sizes[1] * sizes[2]), mid=there // sizes[2] % sizes[1], freq=there % sizes[2])

    return index, total, ahead


def swap_kernel(sizes, with_ids, *refs):
    if with_ids:
        blocks, ids, got, got_ids, own_sem, send_sem, recv_sem, id_own, id_send, id_recv = refs
    else:
        blocks, got, own_sem, send_sem, recv_sem = refs
    index, total, ahead = place(sizes)
    n_off = sizes[0]
    barrier = pltpu.get_barrier_semaphore()

    @pl.loop(1, total)
    def _(i):
        signal(barrier, **ahead(i)[1])

    own = pltpu.make_async_copy(blocks.at[index], got.at[index], own_sem)
    own.start()
    pl.semaphore_wait(barrier, total - 1)

    def block_copy(i):
        there, device = ahead(i)
        return send(blocks.at[there], got.at[index], send_sem.at[i], recv_sem.at[i], **device)

    def id_copy(d):
        off = lax.axis_index("off")
        return send(ids, got_ids.at[off], id_send.at[d], id_recv.at[d], off=(off + d) % n_off)

    if with_ids:
        own_ids = pltpu.make_async_copy(ids, got_ids.at[lax.axis_index("off")], id_own)
        own_ids.start()
        for d in range(1, n_off):
            id_copy(d).start()

    @pl.loop(1, total)
    def _(i):
        block_copy(i).start()

    own.wait()
    if with_ids:
        own_ids.wait()
        for d in range(1, n_off):
            id_copy(d).wait()

    @pl.loop(1, total)
    def _(i):
        block_copy(i).wait()


def swap(blocks, sizes, collective_id, ids=None):
    total, n_off = blocks.shape[0], sizes[0]
    dma = pltpu.SemaphoreType.DMA
    shapes = [jax.ShapeDtypeStruct(blocks.shape, blocks.dtype)]
    scratch = [dma, dma((total,)), dma((total,))]
    operands = [blocks]
    if ids is not None:
        shapes.append(jax.ShapeDtypeStruct((n_off,) + ids.shape, ids.dtype))
        scratch += [dma, dma((n_off,)), dma((n_off,))]
        operands.append(ids)
    return pl.pallas_call(
        functools.partial(swap_kernel, sizes, ids is not None),
        out_shape=shapes,
        in_specs=[VMEM] * len(operands),
        out_specs=[VMEM] * len(shapes),
        scratch_shapes=scratch,
        compiler_params=pltpu.CompilerParams(collective_id=collective_id, has_side_effects=True),
    )(*operands)


def radon_kernel(n_mid, n_off, smooth, level, table, out, weights, sem):
    count, mids = smooth.shape[1:3]
    q = (lax.axis_index("freq") * n_mid + lax.axis_index("mid")) * n_off + lax.axis_index("off")
    fetch = pltpu.make_async_copy(table.at[pl.ds(q * count, count)], weights, sem)
    fetch.start()
    re = smooth[0].astype(jnp.float32)
    im = smooth[1].astype(jnp.float32)
    first = jnp.concatenate([re, -im], axis=2)
    second = jnp.concatenate([im, re], axis=2)
    x = jnp.concatenate([first, second], axis=1).astype(jnp.bfloat16)
    fetch.wait()
    model = lax.dot_general(x, weights[...], (((2,), (1,)), ((0,), (0,))), preferred_element_type=jnp.float32)
    model_re, model_im = model[:, :mids], model[:, mids:]
    power = model_re * model_re + model_im * model_im
    keep = (lax.broadcasted_iota(jnp.int32, power.shape, 2) >= NP // 4).astype(jnp.float32)
    lev = level[...]
    factor = power / (power + lev * lev) * keep
    kept = jnp.concatenate([model_re * factor, model_im * factor], axis=1).astype(jnp.bfloat16)
    both = lax.dot_general(kept, weights[...], (((2,), (2,)), ((0,), (0,))), preferred_element_type=jnp.float32)
    out[0] = (both[:, :mids, :NOFF] + both[:, mids:, NOFF:]).astype(jnp.bfloat16)
    out[1] = (both[:, mids:, :NOFF] - both[:, :mids, NOFF:]).astype(jnp.bfloat16)


def radon(smooth, level, table, n_mid, n_off):
    count = smooth.shape[1]
    return pl.pallas_call(
        functools.partial(radon_kernel, n_mid, n_off),
        out_shape=jax.ShapeDtypeStruct(smooth.shape, jnp.bfloat16),
        in_specs=[VMEM, VMEM, ANY],
        out_specs=VMEM,
        scratch_shapes=[pltpu.VMEM((count, 2 * NOFF, NP), jnp.bfloat16), pltpu.SemaphoreType.DMA],
        compiler_params=pltpu.CompilerParams(vmem_limit_bytes=24 * 1024 * 1024),
    )(smooth, level, table)


def fused_kernel(sizes, traces_hbm, filter_hbm, mid_hbm, off_hbm, level_hbm, dft_hbm, inv_hbm, table_hbm, out, traces, filt, mid_ids, off_ids, level, dft, inv, weights, keys, key_col, near, same, blocks, got, back, ret, routes, cube, lev, load_sem, filt_sem, dft_sem, send_sem, recv_sem, id_send, id_recv):
    n_off, n_mid, n_freq = sizes
    total = n_off * n_mid * n_freq
    off, mid, freq = (lax.axis_index(name) for name in ("off", "mid", "freq"))
    f32, bf16 = jnp.float32, jnp.bfloat16
    lines, wide = blocks.shape[1:]
    width = wide // 2
    count = width // 2
    half = NOFF // n_off
    mids = lev.shape[1]
    cells = mids * half
    per_half = keys.shape[2]
    spacing = 2 * mids
    group = n_off * n_freq * width

    def peer(dm, df, do):
        m, f, o = lax.rem(mid + dm, n_mid), lax.rem(freq + df, n_freq), lax.rem(off + do, n_off)
        return (o * n_mid + m) * n_freq + f, dict(off=o, mid=m, freq=f)

    index = (off * n_mid + mid) * n_freq + freq
    far_first = [3, 1, 2, 0]
    peers = [(dm, df, do) for do in reversed(range(n_off)) for df in reversed(range(n_freq)) for dm in [3, 1, 2, 0]]
    others = [p for p in peers if p != (0, 0, 0)]
    barrier = pltpu.get_barrier_semaphore()
    for p in others:
        signal(barrier, **peer(*p)[1])

    def load(src, dst, sem):
        copy = pltpu.make_async_copy(src, dst, sem)
        copy.start()
        return copy

    span = filt.shape[1] // n_mid
    get_traces = load(traces_hbm, traces, load_sem.at[0])
    get_filter = [
        load(filter_hbm.at[:, pl.ds(i * span, span)], filt.at[:, pl.ds(i * span, span)], filt_sem.at[i])
        for i in range(n_mid)
    ]
    get_mid = load(mid_hbm, mid_ids, load_sem.at[1])
    get_off = load(off_hbm, off_ids, load_sem.at[2])
    get_level = load(level_hbm, level, load_sem.at[3])
    q = (freq * n_mid + mid) * n_off + off
    pairs = weights.shape[0]

    get_traces.wait()
    parts = []
    for i in range(n_mid):
        get_filter[i].wait()
        if i == 0:
            get_dft = [load(dft_hbm.at[m], dft.at[m], dft_sem.at[m]) for m in range(n_mid)]
        part = jnp.dot(traces[...], filt[:, i * span : (i + 1) * span], preferred_element_type=f32)
        parts.append(part.astype(bf16))
    folds = n_mid // 2
    stacked = jnp.concatenate([jnp.concatenate(parts[i * folds :][:folds], axis=1) for i in range(2)], axis=0)
    odd = lax.broadcasted_iota(jnp.int32, (1, group), 1) % 2 == 1
    def id_copy(d):
        return send(keys.at[off], keys.at[off], id_send.at[d], id_recv.at[d], off=lax.rem(off + d, n_off))

    def block_copy(way, src, dst, p):
        there, device = peer(*p)
        slot = (p[2] * n_freq + p[1]) * n_mid + p[0]
        return send(src.at[there], dst.at[index], send_sem.at[way, slot], recv_sem.at[way, slot], **device)

    for get in get_dft:
        get.wait()
    get_weights = load(table_hbm.at[pl.ds(q * pairs, pairs)], weights, load_sem.at[4])
    get_inv = load(inv_hbm, inv, load_sem.at[5])
    low = lax.broadcasted_iota(jnp.int32, (lines, wide), 1) < width
    for m in range(n_mid):
        halves = jnp.dot(stacked, dft[m], preferred_element_type=f32)
        first, second = halves[: 2 * lines], halves[2 * lines :]
        spectra = first + jnp.where(odd, -second, second)
        for i in range(0, n_off * n_freq, 2):
            top, bottom = (spectra[pk * lines :, i * width :][:lines, :wide] for pk in range(2))
            pair = jnp.where(low, top, pltpu.roll(bottom, width, 1)), jnp.where(low, pltpu.roll(top, width, 1), bottom)
            for at in range(2):
                o, f = (i + at) // n_freq, (i + at) % n_freq
                blocks[(o * n_mid + m) * n_freq + f] = pair[at].astype(bf16)
    get_mid.wait()
    get_off.wait()
    keys[off] = (off_ids[...] - off * half) * spacing + mid_ids[...]
    pl.semaphore_wait(barrier, total - 1)
    for d in range(1, n_off):
        id_copy(d).start()
    for p in others:
        block_copy(0, blocks, got, p).start()
    got[index] = blocks[index]

    get_level.wait()
    for k in range(count):
        own_level = level[(mid * n_off + off) * count + k]
        lev[k] = jnp.full((mids, NP), own_level * own_level, f32)
    for d in range(1, n_off):
        id_copy(d).wait_recv()

    def column_key(shape, dim, o):
        col = lax.broadcasted_iota(jnp.int32, shape, dim)
        j, u, h = col // NOFF, col // half % 2, col % half
        return (h * spacing + 2 * j + (u + o) % 2).astype(f32)

    for o in range(n_off):
        key = keys[o].astype(f32)
        n_src = total // n_off
        side = n_src // 2
        pieces = [[key[:, (s * 2 + pk) * lines :][:, :lines] for s in range(n_src)] for pk in range(2)]
        staged = [piece for g in range(2) for pk in range(2) for piece in pieces[pk][g * side : (g + 1) * side]]
        key = jnp.concatenate(staged, axis=1)
        key_col[o] = jnp.transpose(jnp.broadcast_to(key, (NOFF, per_half)))
        col_of_lane = column_key((1, cells), 1, o)
        step = 64

        @pl.loop(0, per_half // step)
        def _(j):
            here = pl.multiple_of(j * step, step)
            own = key_col[o, pl.ds(here, step)]
            own = jnp.concatenate([own] * (cells // NOFF), axis=1)
            away = jnp.abs(own - col_of_lane)
            near[o, pl.ds(here, step)] = jnp.where(away == 0, 0.5, jnp.where(away == 1, 0.25, 0.0)).astype(bf16)

        @pl.loop(0, cells // step)
        def _(j):
            here = pl.multiple_of(j * step, step)
            col = lax.broadcasted_iota(jnp.int32, (step, NOFF), 0) + here
            c, u, h = col // NOFF, col // half % 2, col % half
            col = (h * spacing + 2 * c + (u + o) % 2).astype(f32)
            col = jnp.concatenate([col] * (per_half // NOFF), axis=1)
            same[o, pl.ds(here, step)] = jnp.where(col == key, 1.0, 0.0).astype(bf16)

    get_weights.wait()
    n_src = total // n_off
    side, reach = n_src // 2, n_mid // 2
    near_side = mid // reach
    gathered = [None] * n_off
    for step, g in enumerate((near_side, 1 - near_side)):
        for j in range(reach):
            m = g * reach + (lax.rem(mid + j, reach) if step == 0 else j)
            dm = 0 if step == 0 and j == 0 else lax.rem(mid - m + n_mid, n_mid)
            for df in range(n_freq):
                for do in range(n_off):
                    if step or j or df or do:
                        block_copy(0, blocks, got, (dm, df, do)).wait_recv()
        for o in range(n_off):
            rows = got[pl.ds(o * n_src + g * side, side)].reshape(side * lines, wide)
            rows = jnp.transpose(rows.astype(f32)).astype(bf16)
            rows = jnp.concatenate([rows[:width], rows[width:]], axis=1)
            spot = pl.multiple_of(g * (per_half // 2), per_half // 2)
            part = jnp.dot(rows, near[o, pl.ds(spot, per_half // 2)], preferred_element_type=f32)
            gathered[o] = part if step == 0 else gathered[o] + part
    low = lax.broadcasted_iota(jnp.int32, (width, NOFF), 1) < half
    for j in range(mids // 2):
        a, b = (g[:, j * NOFF : (j + 1) * NOFF] for g in gathered)
        cube[pl.ds(2 * j, width, stride=mids), :] = jnp.where(low, a, b)
        cube[pl.ds(2 * j + 1, width, stride=mids), :] = pltpu.roll(jnp.where(low, b, a), half, 1)
    re, im = cube[...].reshape(2, count, mids, NOFF)
    first = jnp.concatenate([re, -im], axis=2)
    second = jnp.concatenate([im, re], axis=2)
    x = jnp.concatenate([first, second], axis=1).astype(bf16).reshape(pairs, 4 * mids, 2 * NOFF)
    both = lax.dot_general(x, weights[...], (((2,), (1,)), ((0,), (0,))), preferred_element_type=f32)
    keep = (lax.broadcasted_iota(jnp.int32, (mids, NP), 1) >= NP // 4).astype(f32)
    levels = lev[...].reshape(pairs, 2, mids, NP)
    kept = []
    for i in range(2):
        model_re = both[:, 2 * i * mids : (2 * i + 1) * mids, i * NP : (i + 1) * NP]
        model_im = both[:, (2 * i + 1) * mids : (2 * i + 2) * mids, i * NP : (i + 1) * NP]
        power = model_re * model_re + model_im * model_im
        factor = power / (power + levels[:, i]) * keep
        part = jnp.concatenate([model_re * factor, model_im * factor], axis=1)
        blank = jnp.zeros_like(part)
        kept.append(jnp.concatenate([blank] * i + [part] + [blank] * (1 - i), axis=2))
    kept = jnp.concatenate(kept, axis=1).astype(bf16)
    both = lax.dot_general(kept, weights[...], (((2,), (2,)), ((0,), (0,))), preferred_element_type=f32)
    both = both.reshape(count, 2 * mids, 2 * NOFF)
    mult_re = both[:, :mids, :NOFF] + both[:, mids:, NOFF:]
    mult_im = both[:, mids:, :NOFF] - both[:, :mids, NOFF:]
    cube[...] = jnp.concatenate([mult_re, mult_im], axis=0).reshape(width * mids, NOFF)
    mult = [[], []]
    for j in range(mids // 2):
        even = cube[pl.ds(2 * j, width, stride=mids), :]
        other = pltpu.roll(cube[pl.ds(2 * j + 1, width, stride=mids), :], half, 1)
        mult[0].append(jnp.where(low, even, other))
        mult[1].append(jnp.where(low, other, even))
    for o in range(n_off):
        routes[o] = jnp.concatenate(mult[o], axis=1).astype(bf16)
    for step, g in enumerate((1 - near_side, near_side)):
        spot = pl.multiple_of(g * (per_half // 2), per_half // 2)
        for o in range(n_off):
            routed = jnp.dot(routes[o], same[o, :, pl.ds(spot, per_half // 2)], preferred_element_type=f32)
            routed = jnp.concatenate([routed[:, : per_half // 4], routed[:, per_half // 4 :]], axis=0)
            back[pl.ds(o * n_src + g * side, side)] = jnp.transpose(routed).astype(bf16).reshape(side, lines, wide)
        for do in reversed(range(n_off)):
            for df in reversed(range(n_freq)):
                for j in range(reach):
                    m = g * reach + (j if step == 0 else lax.rem(mid + j, reach))
                    dm = 0 if step and j == 0 else lax.rem(m - mid + n_mid, n_mid)
                    if step == 0 or j or df or do:
                        block_copy(1, back, ret, (dm, df, do)).start()
    ret[index] = back[index]

    get_inv.wait()
    low = lax.broadcasted_iota(jnp.int32, (lines, wide), 1) < width
    total_out = None
    for dm in reversed(far_first):
        m = lax.rem(mid + dm, n_mid)
        for p in others:
            if (p[0] + dm) % n_mid == 0:
                block_copy(1, back, ret, p).wait_recv()
        clean = []
        for o in range(n_off):
            for f in range(n_freq):
                d = (o * n_mid + m) * n_freq + f
                clean.append(blocks[d].astype(f32) - ret[d].astype(f32))
        top, bottom = [], []
        for i in range(0, len(clean), 2):
            top.append(jnp.where(low, clean[i], pltpu.roll(clean[i + 1], width, 1)))
            bottom.append(jnp.where(low, pltpu.roll(clean[i], width, 1), clean[i + 1]))
        clean = jnp.concatenate([jnp.concatenate(top, axis=1), jnp.concatenate(bottom, axis=1)], axis=0)
        clean = jnp.concatenate([clean, jnp.where(odd, -clean, clean)], axis=0).astype(bf16)
        sums = jnp.dot(clean, inv[m], preferred_element_type=f32)
        total_out = sums if total_out is None else total_out + sums
    n_time = inv.shape[2]
    out[:, :n_time] = total_out[: 2 * lines].astype(bf16)
    out[:, n_time:] = total_out[2 * lines :].astype(bf16)
    for way, src, dst in ((0, blocks, got), (1, back, ret)):
        for p in others:
            block_copy(way, src, dst, p).wait_send()
    for d in range(1, n_off):
        id_copy(d).wait_send()


def fused(traces, time_filter, midpoint_of, offset_of, level, dft, inv, table, sizes):
    n_off, n_mid, n_freq = sizes
    total = n_off * n_mid * n_freq
    count = level.shape[0] // (n_mid * n_off)
    width = 2 * count
    lines = traces.shape[0] // 2
    per_half = midpoint_of.shape[1]
    mids = n_off * per_half // NOFF
    cells = per_half
    dma = pltpu.SemaphoreType.DMA
    f32, bf16, i32 = jnp.float32, jnp.bfloat16, jnp.int32
    shape = (total, lines, 2 * width)
    hbm = pl.BlockSpec(memory_space=pltpu.HBM)
    operands = (traces, time_filter, midpoint_of, offset_of, level, dft, inv, table)
    return pl.pallas_call(
        functools.partial(fused_kernel, sizes),
        out_shape=jax.ShapeDtypeStruct(traces.shape, traces.dtype),
        in_specs=[hbm] * 8,
        out_specs=VMEM,
        scratch_shapes=[
            pltpu.VMEM(traces.shape, bf16),
            pltpu.VMEM(time_filter.shape, bf16),
            pltpu.VMEM(midpoint_of.shape, i32),
            pltpu.VMEM(offset_of.shape, i32),
            pltpu.SMEM(level.shape, f32),
            pltpu.VMEM(dft.shape, bf16),
            pltpu.VMEM(inv.shape, bf16),
            pltpu.VMEM((count // 2,) + table.shape[1:], bf16),
            pltpu.VMEM((n_off, 1, per_half), i32),
            pltpu.VMEM((n_off, per_half, NOFF), f32),
            pltpu.VMEM((n_off, per_half, cells), bf16),
            pltpu.VMEM((n_off, cells, per_half), bf16),
            pltpu.VMEM(shape, bf16),
            pltpu.VMEM(shape, bf16),
            pltpu.VMEM(shape, bf16),
            pltpu.VMEM(shape, bf16),
            pltpu.VMEM((n_off, width, cells), bf16),
            pltpu.VMEM((width * mids, NOFF), f32),
            pltpu.VMEM((count, mids, NP), f32),
            dma((6,)),
            dma((n_mid,)),
            dma((n_mid,)),
            dma((2, total)),
            dma((2, total)),
            dma((n_off,)),
            dma((n_off,)),
        ],
        compiler_params=pltpu.CompilerParams(
            collective_id=2, has_side_effects=True, vmem_limit_bytes=32 * 1024 * 1024
        ),
    )(*(pltpu.with_memory_space_constraint(x, pltpu.HBM) for x in operands))


def small(n_traces, n_off, width):
    return n_traces <= 4096 and n_off == 2 and width == 64


def on_device(dft, inv, weights, traces, time_filter, midpoint_of, offset_of, shrink_level):
    n_mid = lax.axis_size("mid")
    n_freq = lax.axis_size("freq")
    n_off = lax.axis_size("off")
    sizes = (n_off, n_mid, n_freq)
    total = n_off * n_mid * n_freq
    me_mid = lax.axis_index("mid")
    me_off = lax.axis_index("off")
    tr_dev = traces.shape[1]
    count = shrink_level.shape[0] // (n_mid * n_off)
    width = 2 * count
    pack = max(1, min(tr_dev, 128 // width))
    n_traces = total * tr_dev
    n_mids = n_traces // NOFF
    f32, bf16 = jnp.float32, jnp.bfloat16

    if small(n_traces, n_off, width):
        return fused(traces[0], time_filter, midpoint_of, offset_of, shrink_level, dft, inv, weights, sizes)[None]
    own_ids = midpoint_of * NOFF + offset_of
    filtered = jnp.dot(traces[0], time_filter, preferred_element_type=f32).astype(bf16)
    spectra = jnp.dot(filtered, dft, preferred_element_type=f32).astype(bf16)
    blocks = spectra.reshape(pack, tr_dev // pack, total, width)
    blocks = jnp.transpose(blocks, (2, 1, 0, 3)).reshape(total, tr_dev // pack, pack * width)
    own_levels = lax.dynamic_slice_in_dim(shrink_level, (me_mid * n_off + me_off) * count, count)
    level = jnp.broadcast_to(own_levels[:, None, None], (count, 1, NP))
    rows, ids = swap(blocks, sizes, 0, own_ids)
    rows = rows.reshape(total, tr_dev // pack, pack, width)
    rows = jnp.transpose(rows, (0, 2, 1, 3)).reshape(n_traces, width)
    cell_of = ids.reshape(n_traces)
    gather = jnp.zeros((n_traces, width), bf16).at[cell_of].set(rows)
    edged = jnp.pad(gather.reshape(n_mids, NOFF, 2, count).astype(f32), ((1, 1), (0, 0), (0, 0), (0, 0)))
    smooth = ((edged[:-2] + 2.0 * edged[1:-1] + edged[2:]) * 0.25).astype(bf16)
    smooth = jnp.transpose(smooth, (2, 3, 0, 1))
    mult = radon(smooth, level, weights, n_mid, n_off).reshape(width, n_traces)
    back = jnp.transpose(mult)[cell_of].reshape(total, pack, tr_dev // pack, width)
    back = jnp.transpose(back, (0, 2, 1, 3)).reshape(total, tr_dev // pack, pack * width)
    (returned,) = swap(back, sizes, 1)
    returned = returned.reshape(total, tr_dev // pack, pack, width)
    own_mult = jnp.transpose(returned, (2, 1, 0, 3)).reshape(tr_dev, total * width)
    clean = (spectra.astype(f32) - own_mult.astype(f32)).astype(bf16)
    sums = lax.dot_general(clean, dft, (((1,), (1,)), ((), ())), preferred_element_type=f32)
    return (2.0 * sums).astype(bf16)[None]


def solution(mesh):
    n_freq, n_mid, n_off = (mesh.shape[name] for name in ("freq", "mid", "off"))

    def run(traces, time_filter, midpoint_of, offset_of, shrink_level):
        n_freqs = shrink_level.shape[0]
        n_time = traces.shape[2]
        pieces = n_freq * n_mid * n_off
        count = n_freqs // pieces
        dft = dft_table(n_time, pieces, count).reshape(n_time, n_freq, n_mid, n_off, -1)
        weights = radon_table(n_freqs)
        part_traces = traces.shape[0] * traces.shape[1] // mesh.shape["group"]
        if small(part_traces, n_off, 2 * count):
            dft = np.ascontiguousarray(dft[: n_time // 2].transpose(2, 0, 3, 1, 4)).reshape(n_mid, n_time // 2, -1)
            inv = np.ascontiguousarray(dft.transpose(0, 2, 1)) * np.asarray(2, dft.dtype)
            weights = weights.reshape(n_freqs // 2, 2, 2 * NOFF, NP).transpose(0, 2, 1, 3)
            weights = np.ascontiguousarray(weights).reshape(n_freqs // 2, 2 * NOFF, 2 * NP)
        else:
            dft = np.ascontiguousarray(dft.transpose(0, 3, 2, 1, 4)).reshape(n_time, 2 * n_freqs)
            inv = np.zeros((1,), dft.dtype)
        return jax.shard_map(
            on_device,
            mesh=mesh,
            in_specs=(
                P(),
                P(),
                P(),
                P("off", ("group", "mid", "freq"), None),
                P(),
                P("off", "group"),
                P("off", "group"),
                P("freq"),
            ),
            out_specs=P("off", ("group", "mid", "freq"), None),
            check_vma=False,
        )(jnp.asarray(dft), jnp.asarray(inv), jnp.asarray(weights), traces, time_filter, midpoint_of, offset_of, shrink_level)

    return run
```

```python
import functools
import math

import jax
import jax.numpy as jnp
import numpy as np
from jax import lax
from jax.experimental import pallas as pl
from jax.experimental.pallas import tpu as pltpu
from jax.sharding import PartitionSpec as P

NOFF = 128
NP = 128
radon_period = 4096
VMEM = pl.BlockSpec(memory_space=pltpu.VMEM)
ANY = pl.BlockSpec(memory_space=pl.ANY)


def dft_table(n_time, n_bands, band_size):
    sample = np.arange(n_time, dtype=np.int64)[:, None]
    freq_index = np.arange(n_bands * band_size, dtype=np.int64)[None, :]
    angle = 2.0 * np.pi * (sample * freq_index % n_time) / n_time
    scale_f = 1.0 / math.sqrt(n_time)
    cosine = (np.cos(angle) * scale_f).reshape(n_time, n_bands, band_size)
    sine = (-np.sin(angle) * scale_f).reshape(n_time, n_bands, band_size)
    table = np.stack([cosine, sine], axis=2).reshape(n_time, n_bands * 2 * band_size)
    return table.astype(np.float32).astype(jnp.bfloat16)


def radon_table(n_freqs):
    freq_index = np.arange(n_freqs, dtype=np.int64)[:, None, None]
    offset_index = np.arange(NOFF, dtype=np.int64)[None, :, None]
    slowness = np.arange(NP, dtype=np.int64)[None, None, :]
    turns = freq_index * slowness % radon_period * (offset_index * offset_index % radon_period) % radon_period
    circle = 2.0 * np.pi * np.arange(radon_period) / radon_period
    scale_r = 1.0 / math.sqrt(NOFF)
    cosine = (np.cos(circle) * scale_r).astype(np.float32).astype(jnp.bfloat16)[turns]
    sine = (np.sin(circle) * scale_r).astype(np.float32).astype(jnp.bfloat16)[turns]
    return np.stack([cosine, sine], axis=1).reshape(n_freqs, 2 * NOFF, NP)


def signal(barrier, **device):
    pl.semaphore_signal(barrier, inc=1, device_id=device, device_id_type=pl.DeviceIdType.MESH)


def send(src, dst, send_sem, recv_sem, **device):
    return pltpu.make_async_remote_copy(
        src_ref=src,
        dst_ref=dst,
        send_sem=send_sem,
        recv_sem=recv_sem,
        device_id=device,
        device_id_type=pl.DeviceIdType.MESH,
    )


def place(sizes):
    names = ("off", "mid", "freq")
    here = [lax.axis_index(name) for name in names]
    index = (here[0] * sizes[1] + here[1]) * sizes[2] + here[2]
    total = sizes[0] * sizes[1] * sizes[2]

    def ahead(i):
        there = (index + i) % total
        return there, dict(off=there // (sizes[1] * sizes[2]), mid=there // sizes[2] % sizes[1], freq=there % sizes[2])

    return index, total, ahead


def swap_kernel(sizes, with_ids, *refs):
    if with_ids:
        blocks, ids, got, got_ids, own_sem, send_sem, recv_sem, id_own, id_send, id_recv = refs
    else:
        blocks, got, own_sem, send_sem, recv_sem = refs
    index, total, ahead = place(sizes)
    n_off = sizes[0]
    barrier = pltpu.get_barrier_semaphore()

    @pl.loop(1, total)
    def _(i):
        signal(barrier, **ahead(i)[1])

    own = pltpu.make_async_copy(blocks.at[index], got.at[index], own_sem)
    own.start()
    pl.semaphore_wait(barrier, total - 1)

    def block_copy(i):
        there, device = ahead(i)
        return send(blocks.at[there], got.at[index], send_sem.at[i], recv_sem.at[i], **device)

    def id_copy(d):
        off = lax.axis_index("off")
        return send(ids, got_ids.at[off], id_send.at[d], id_recv.at[d], off=(off + d) % n_off)

    if with_ids:
        own_ids = pltpu.make_async_copy(ids, got_ids.at[lax.axis_index("off")], id_own)
        own_ids.start()
        for d in range(1, n_off):
            id_copy(d).start()

    @pl.loop(1, total)
    def _(i):
        block_copy(i).start()

    own.wait()
    if with_ids:
        own_ids.wait()
        for d in range(1, n_off):
            id_copy(d).wait()

    @pl.loop(1, total)
    def _(i):
        block_copy(i).wait()


def swap(blocks, sizes, collective_id, ids=None):
    total, n_off = blocks.shape[0], sizes[0]
    dma = pltpu.SemaphoreType.DMA
    shapes = [jax.ShapeDtypeStruct(blocks.shape, blocks.dtype)]
    scratch = [dma, dma((total,)), dma((total,))]
    operands = [blocks]
    if ids is not None:
        shapes.append(jax.ShapeDtypeStruct((n_off,) + ids.shape, ids.dtype))
        scratch += [dma, dma((n_off,)), dma((n_off,))]
        operands.append(ids)
    return pl.pallas_call(
        functools.partial(swap_kernel, sizes, ids is not None),
        out_shape=shapes,
        in_specs=[VMEM] * len(operands),
        out_specs=[VMEM] * len(shapes),
        scratch_shapes=scratch,
        compiler_params=pltpu.CompilerParams(collective_id=collective_id, has_side_effects=True),
    )(*operands)


def radon_kernel(n_mid, n_off, smooth, level, table, out, weights, sem):
    count, mids = smooth.shape[1:3]
    q = (lax.axis_index("freq") * n_mid + lax.axis_index("mid")) * n_off + lax.axis_index("off")
    fetch = pltpu.make_async_copy(table.at[pl.ds(q * count, count)], weights, sem)
    fetch.start()
    re = smooth[0].astype(jnp.float32)
    im = smooth[1].astype(jnp.float32)
    first = jnp.concatenate([re, -im], axis=2)
    second = jnp.concatenate([im, re], axis=2)
    x = jnp.concatenate([first, second], axis=1).astype(jnp.bfloat16)
    fetch.wait()
    model = lax.dot_general(x, weights[...], (((2,), (1,)), ((0,), (0,))), preferred_element_type=jnp.float32)
    model_re, model_im = model[:, :mids], model[:, mids:]
    power = model_re * model_re + model_im * model_im
    keep = (lax.broadcasted_iota(jnp.int32, power.shape, 2) >= NP // 4).astype(jnp.float32)
    lev = level[...]
    factor = power / (power + lev * lev) * keep
    kept = jnp.concatenate([model_re * factor, model_im * factor], axis=1).astype(jnp.bfloat16)
    both = lax.dot_general(kept, weights[...], (((2,), (2,)), ((0,), (0,))), preferred_element_type=jnp.float32)
    out[0] = (both[:, :mids, :NOFF] + both[:, mids:, NOFF:]).astype(jnp.bfloat16)
    out[1] = (both[:, mids:, :NOFF] - both[:, :mids, NOFF:]).astype(jnp.bfloat16)


def radon(smooth, level, table, n_mid, n_off):
    count = smooth.shape[1]
    return pl.pallas_call(
        functools.partial(radon_kernel, n_mid, n_off),
        out_shape=jax.ShapeDtypeStruct(smooth.shape, jnp.bfloat16),
        in_specs=[VMEM, VMEM, ANY],
        out_specs=VMEM,
        scratch_shapes=[pltpu.VMEM((count, 2 * NOFF, NP), jnp.bfloat16), pltpu.SemaphoreType.DMA],
        compiler_params=pltpu.CompilerParams(vmem_limit_bytes=24 * 1024 * 1024),
    )(smooth, level, table)


def fused_kernel(sizes, traces_hbm, filter_hbm, mid_hbm, off_hbm, level_hbm, dft_hbm, inv_hbm, table_hbm, out, traces, filt, mid_ids, off_ids, level, dft, inv, weights, keys, key_col, near, same, blocks, got, back, ret, routes, cube, lev, load_sem, filt_sem, dft_sem, send_sem, recv_sem, id_send, id_recv):
    n_off, n_mid, n_freq = sizes
    total = n_off * n_mid * n_freq
    off, mid, freq = (lax.axis_index(name) for name in ("off", "mid", "freq"))
    f32, bf16 = jnp.float32, jnp.bfloat16
    lines, wide = blocks.shape[1:]
    width = wide // 2
    count = width // 2
    half = NOFF // n_off
    mids = lev.shape[1]
    cells = mids * half
    per_half = keys.shape[2]
    spacing = 2 * mids
    group = n_off * n_freq * width

    def peer(dm, df, do):
        m, f, o = lax.rem(mid + dm, n_mid), lax.rem(freq + df, n_freq), lax.rem(off + do, n_off)
        return (o * n_mid + m) * n_freq + f, dict(off=o, mid=m, freq=f)

    index = (off * n_mid + mid) * n_freq + freq
    far_first = sorted(range(n_mid), key=lambda dm: (dm == 0, min(dm, n_mid - dm), -dm))
    peers = [(dm, df, do) for do in reversed(range(n_off)) for df in reversed(range(n_freq)) for dm in far_first]
    others = [p for p in peers if p != (0, 0, 0)]
    barrier = pltpu.get_barrier_semaphore()
    for p in others:
        signal(barrier, **peer(*p)[1])

    def load(src, dst, sem):
        copy = pltpu.make_async_copy(src, dst, sem)
        copy.start()
        return copy

    span = filt.shape[1] // n_mid
    get_traces = load(traces_hbm, traces, load_sem.at[0])
    get_filter = [
        load(filter_hbm.at[:, pl.ds(i * span, span)], filt.at[:, pl.ds(i * span, span)], filt_sem.at[i])
        for i in range(n_mid)
    ]
    get_mid = load(mid_hbm, mid_ids, load_sem.at[1])
    get_off = load(off_hbm, off_ids, load_sem.at[2])
    get_level = load(level_hbm, level, load_sem.at[3])
    q = (freq * n_mid + mid) * n_off + off
    pairs = weights.shape[0]

    get_traces.wait()
    parts = []
    for i in range(n_mid):
        get_filter[i].wait()
        if i == 0:
            get_dft = [load(dft_hbm.at[m], dft.at[m], dft_sem.at[m]) for m in range(n_mid)]
        part = jnp.dot(traces[...], filt[:, i * span : (i + 1) * span], preferred_element_type=f32)
        parts.append(part.astype(bf16))
    folds = n_mid // 2
    stacked = jnp.concatenate([jnp.concatenate(parts[i * folds :][:folds], axis=1) for i in range(2)], axis=0)
    odd = lax.broadcasted_iota(jnp.int32, (1, group), 1) % 2 == 1
    def id_copy(d):
        return send(keys.at[off], keys.at[off], id_send.at[d], id_recv.at[d], off=lax.rem(off + d, n_off))

    def block_copy(way, src, dst, p):
        there, device = peer(*p)
        slot = (p[2] * n_freq + p[1]) * n_mid + p[0]
        return send(src.at[there], dst.at[index], send_sem.at[way, slot], recv_sem.at[way, slot], **device)

    for get in get_dft:
        get.wait()
    get_weights = load(table_hbm.at[pl.ds(q * pairs, pairs)], weights, load_sem.at[4])
    get_inv = load(inv_hbm, inv, load_sem.at[5])
    low = lax.broadcasted_iota(jnp.int32, (lines, wide), 1) < width
    for m in range(n_mid):
        halves = jnp.dot(stacked, dft[m], preferred_element_type=f32)
        first, second = halves[: 2 * lines], halves[2 * lines :]
        spectra = first + jnp.where(odd, -second, second)
        for i in range(0, n_off * n_freq, 2):
            top, bottom = (spectra[pk * lines :, i * width :][:lines, :wide] for pk in range(2))
            pair = jnp.where(low, top, pltpu.roll(bottom, width, 1)), jnp.where(low, pltpu.roll(top, width, 1), bottom)
            for at in range(2):
                o, f = (i + at) // n_freq, (i + at) % n_freq
                blocks[(o * n_mid + m) * n_freq + f] = pair[at].astype(bf16)
    get_mid.wait()
    get_off.wait()
    keys[off] = (off_ids[...] - off * half) * spacing + mid_ids[...]
    pl.semaphore_wait(barrier, total - 1)
    for d in range(1, n_off):
        id_copy(d).start()
    for p in others:
        block_copy(0, blocks, got, p).start()
    got[index] = blocks[index]

    get_level.wait()
    for k in range(count):
        own_level = level[(mid * n_off + off) * count + k]
        lev[k] = jnp.full((mids, NP), own_level * own_level, f32)
    for d in range(1, n_off):
        id_copy(d).wait_recv()

    def column_key(shape, dim, o):
        col = lax.broadcasted_iota(jnp.int32, shape, dim)
        j, u, h = col // NOFF, col // half % 2, col % half
        return (h * spacing + 2 * j + (u + o) % 2).astype(f32)

    for o in range(n_off):
        key = keys[o].astype(f32)
        n_src = total // n_off
        side = n_src // 2
        pieces = [[key[:, (s * 2 + pk) * lines :][:, :lines] for s in range(n_src)] for pk in range(2)]
        staged = [piece for g in range(2) for pk in range(2) for piece in pieces[pk][g * side : (g + 1) * side]]
        key = jnp.concatenate(staged, axis=1)
        key_col[o] = jnp.transpose(jnp.broadcast_to(key, (NOFF, per_half)))
        col_of_lane = column_key((1, cells), 1, o)
        step = 64

        @pl.loop(0, per_half // step)
        def _(j):
            here = pl.multiple_of(j * step, step)
            own = key_col[o, pl.ds(here, step)]
            own = jnp.concatenate([own] * (cells // NOFF), axis=1)
            away = jnp.abs(own - col_of_lane)
            near[o, pl.ds(here, step)] = jnp.where(away == 0, 0.5, jnp.where(away == 1, 0.25, 0.0)).astype(bf16)

        @pl.loop(0, cells // step)
        def _(j):
            here = pl.multiple_of(j * step, step)
            col = lax.broadcasted_iota(jnp.int32, (step, NOFF), 0) + here
            c, u, h = col // NOFF, col // half % 2, col % half
            col = (h * spacing + 2 * c + (u + o) % 2).astype(f32)
            col = jnp.concatenate([col] * (per_half // NOFF), axis=1)
            same[o, pl.ds(here, step)] = jnp.where(col == key, 1.0, 0.0).astype(bf16)

    get_weights.wait()
    n_src = total // n_off
    side, reach = n_src // 2, n_mid // 2
    near_side = mid // reach
    gathered = [None] * n_off
    for step, g in enumerate((near_side, 1 - near_side)):
        for j in range(reach):
            m = g * reach + (lax.rem(mid + j, reach) if step == 0 else j)
            dm = 0 if step == 0 and j == 0 else lax.rem(mid - m + n_mid, n_mid)
            for df in range(n_freq):
                for do in range(n_off):
                    if step or j or df or do:
                        block_copy(0, blocks, got, (dm, df, do)).wait_recv()
        for o in range(n_off):
            rows = got[pl.ds(o * n_src + g * side, side)].reshape(side * lines, wide)
            rows = jnp.transpose(rows.astype(f32)).astype(bf16)
            rows = jnp.concatenate([rows[:width], rows[width:]], axis=1)
            spot = pl.multiple_of(g * (per_half // 2), per_half // 2)
            part = jnp.dot(rows, near[o, pl.ds(spot, per_half // 2)], preferred_element_type=f32)
            gathered[o] = part if step == 0 else gathered[o] + part
    low = lax.broadcasted_iota(jnp.int32, (width, NOFF), 1) < half
    for j in range(mids // 2):
        a, b = (g[:, j * NOFF : (j + 1) * NOFF] for g in gathered)
        cube[pl.ds(2 * j, width, stride=mids), :] = jnp.where(low, a, b)
        cube[pl.ds(2 * j + 1, width, stride=mids), :] = pltpu.roll(jnp.where(low, b, a), half, 1)
    re, im = cube[...].reshape(2, count, mids, NOFF)
    first = jnp.concatenate([re, -im], axis=2)
    second = jnp.concatenate([im, re], axis=2)
    x = jnp.concatenate([first, second], axis=1).astype(bf16).reshape(pairs, 4 * mids, 2 * NOFF)
    both = lax.dot_general(x, weights[...], (((2,), (1,)), ((0,), (0,))), preferred_element_type=f32)
    keep = (lax.broadcasted_iota(jnp.int32, (mids, NP), 1) >= NP // 4).astype(f32)
    levels = lev[...].reshape(pairs, 2, mids, NP)
    kept = []
    for i in range(2):
        model_re = both[:, 2 * i * mids : (2 * i + 1) * mids, i * NP : (i + 1) * NP]
        model_im = both[:, (2 * i + 1) * mids : (2 * i + 2) * mids, i * NP : (i + 1) * NP]
        power = model_re * model_re + model_im * model_im
        factor = power / (power + levels[:, i]) * keep
        part = jnp.concatenate([model_re * factor, model_im * factor], axis=1)
        blank = jnp.zeros_like(part)
        kept.append(jnp.concatenate([blank] * i + [part] + [blank] * (1 - i), axis=2))
    kept = jnp.concatenate(kept, axis=1).astype(bf16)
    both = lax.dot_general(kept, weights[...], (((2,), (2,)), ((0,), (0,))), preferred_element_type=f32)
    both = both.reshape(count, 2 * mids, 2 * NOFF)
    mult_re = both[:, :mids, :NOFF] + both[:, mids:, NOFF:]
    mult_im = both[:, mids:, :NOFF] - both[:, :mids, NOFF:]
    cube[...] = jnp.concatenate([mult_re, mult_im], axis=0).reshape(width * mids, NOFF)
    mult = [[], []]
    for j in range(mids // 2):
        even = cube[pl.ds(2 * j, width, stride=mids), :]
        other = pltpu.roll(cube[pl.ds(2 * j + 1, width, stride=mids), :], half, 1)
        mult[0].append(jnp.where(low, even, other))
        mult[1].append(jnp.where(low, other, even))
    for o in range(n_off):
        routes[o] = jnp.concatenate(mult[o], axis=1).astype(bf16)
    for step, g in enumerate((1 - near_side, near_side)):
        spot = pl.multiple_of(g * (per_half // 2), per_half // 2)
        for o in range(n_off):
            routed = jnp.dot(routes[o], same[o, :, pl.ds(spot, per_half // 2)], preferred_element_type=f32)
            routed = jnp.concatenate([routed[:, : per_half // 4], routed[:, per_half // 4 :]], axis=0)
            back[pl.ds(o * n_src + g * side, side)] = jnp.transpose(routed).astype(bf16).reshape(side, lines, wide)
        for j in range(reach):
            for do in range(n_off):
                for df in reversed(range(n_freq)):
                    m = g * reach + (j if step == 0 else lax.rem(mid + j, reach))
                    dm = 0 if step and j == 0 else lax.rem(m - mid + n_mid, n_mid)
                    if step == 0 or j or df or do:
                        block_copy(1, back, ret, (dm, df, do)).start()
    ret[index] = back[index]
    for p in others:
        block_copy(0, blocks, got, p).wait_send()
    for d in range(1, n_off):
        id_copy(d).wait_send()

    get_inv.wait()
    low = lax.broadcasted_iota(jnp.int32, (lines, wide), 1) < width
    total_out = None
    for dm in reversed(far_first):
        m = lax.rem(mid + dm, n_mid)
        if dm == far_first[0]:
            for p in others:
                block_copy(1, back, ret, p).wait_send()
        for p in others:
            if (p[0] + dm) % n_mid == 0:
                block_copy(1, back, ret, p).wait_recv()
        clean = []
        for o in range(n_off):
            for f in range(n_freq):
                d = (o * n_mid + m) * n_freq + f
                clean.append(blocks[d].astype(f32) - ret[d].astype(f32))
        top, bottom = [], []
        for i in range(0, len(clean), 2):
            top.append(jnp.where(low, clean[i], pltpu.roll(clean[i + 1], width, 1)))
            bottom.append(jnp.where(low, pltpu.roll(clean[i], width, 1), clean[i + 1]))
        clean = jnp.concatenate([jnp.concatenate(top, axis=1), jnp.concatenate(bottom, axis=1)], axis=0)
        clean = jnp.concatenate([clean, jnp.where(odd, -clean, clean)], axis=0).astype(bf16)
        sums = jnp.dot(clean, inv[m], preferred_element_type=f32)
        total_out = sums if total_out is None else total_out + sums
    n_time = inv.shape[2]
    out[:, :n_time] = total_out[: 2 * lines].astype(bf16)
    out[:, n_time:] = total_out[2 * lines :].astype(bf16)


def fused(traces, time_filter, midpoint_of, offset_of, level, dft, inv, table, sizes):
    n_off, n_mid, n_freq = sizes
    total = n_off * n_mid * n_freq
    count = level.shape[0] // (n_mid * n_off)
    width = 2 * count
    lines = traces.shape[0] // 2
    per_half = midpoint_of.shape[1]
    mids = n_off * per_half // NOFF
    cells = per_half
    dma = pltpu.SemaphoreType.DMA
    f32, bf16, i32 = jnp.float32, jnp.bfloat16, jnp.int32
    shape = (total, lines, 2 * width)
    hbm = pl.BlockSpec(memory_space=pltpu.HBM)
    operands = (traces, time_filter, midpoint_of, offset_of, level, dft, inv, table)
    return pl.pallas_call(
        functools.partial(fused_kernel, sizes),
        out_shape=jax.ShapeDtypeStruct(traces.shape, traces.dtype),
        in_specs=[hbm] * 8,
        out_specs=VMEM,
        scratch_shapes=[
            pltpu.VMEM(traces.shape, bf16),
            pltpu.VMEM(time_filter.shape, bf16),
            pltpu.VMEM(midpoint_of.shape, i32),
            pltpu.VMEM(offset_of.shape, i32),
            pltpu.SMEM(level.shape, f32),
            pltpu.VMEM(dft.shape, bf16),
            pltpu.VMEM(inv.shape, bf16),
            pltpu.VMEM((count // 2,) + table.shape[1:], bf16),
            pltpu.VMEM((n_off, 1, per_half), i32),
            pltpu.VMEM((n_off, per_half, NOFF), f32),
            pltpu.VMEM((n_off, per_half, cells), bf16),
            pltpu.VMEM((n_off, cells, per_half), bf16),
            pltpu.VMEM(shape, bf16),
            pltpu.VMEM(shape, bf16),
            pltpu.VMEM(shape, bf16),
            pltpu.VMEM(shape, bf16),
            pltpu.VMEM((n_off, width, cells), bf16),
            pltpu.VMEM((width * mids, NOFF), f32),
            pltpu.VMEM((count, mids, NP), f32),
            dma((6,)),
            dma((n_mid,)),
            dma((n_mid,)),
            dma((2, total)),
            dma((2, total)),
            dma((n_off,)),
            dma((n_off,)),
        ],
        compiler_params=pltpu.CompilerParams(
            collective_id=2, has_side_effects=True, vmem_limit_bytes=32 * 1024 * 1024
        ),
    )(*(pltpu.with_memory_space_constraint(x, pltpu.HBM) for x in operands))


def small(n_traces, n_off, n_mid, width):
    return n_traces <= 4096 and n_off == 2 and n_mid % 2 == 0 and width == 64


def on_device(dft, inv, weights, traces, time_filter, midpoint_of, offset_of, shrink_level):
    n_mid = lax.axis_size("mid")
    n_freq = lax.axis_size("freq")
    n_off = lax.axis_size("off")
    sizes = (n_off, n_mid, n_freq)
    total = n_off * n_mid * n_freq
    me_mid = lax.axis_index("mid")
    me_off = lax.axis_index("off")
    tr_dev = traces.shape[1]
    count = shrink_level.shape[0] // (n_mid * n_off)
    width = 2 * count
    pack = max(1, min(tr_dev, 128 // width))
    n_traces = total * tr_dev
    n_mids = n_traces // NOFF
    f32, bf16 = jnp.float32, jnp.bfloat16

    if small(n_traces, n_off, n_mid, width):
        return fused(traces[0], time_filter, midpoint_of, offset_of, shrink_level, dft, inv, weights, sizes)[None]
    own_ids = midpoint_of * NOFF + offset_of
    filtered = jnp.dot(traces[0], time_filter, preferred_element_type=f32).astype(bf16)
    spectra = jnp.dot(filtered, dft, preferred_element_type=f32).astype(bf16)
    blocks = spectra.reshape(pack, tr_dev // pack, total, width)
    blocks = jnp.transpose(blocks, (2, 1, 0, 3)).reshape(total, tr_dev // pack, pack * width)
    own_levels = lax.dynamic_slice_in_dim(shrink_level, (me_mid * n_off + me_off) * count, count)
    level = jnp.broadcast_to(own_levels[:, None, None], (count, 1, NP))
    rows, ids = swap(blocks, sizes, 0, own_ids)
    rows = rows.reshape(total, tr_dev // pack, pack, width)
    rows = jnp.transpose(rows, (0, 2, 1, 3)).reshape(n_traces, width)
    cell_of = ids.reshape(n_traces)
    gather = jnp.zeros((n_traces, width), bf16).at[cell_of].set(rows)
    edged = jnp.pad(gather.reshape(n_mids, NOFF, 2, count).astype(f32), ((1, 1), (0, 0), (0, 0), (0, 0)))
    smooth = ((edged[:-2] + 2.0 * edged[1:-1] + edged[2:]) * 0.25).astype(bf16)
    smooth = jnp.transpose(smooth, (2, 3, 0, 1))
    mult = radon(smooth, level, weights, n_mid, n_off).reshape(width, n_traces)
    back = jnp.transpose(mult)[cell_of].reshape(total, pack, tr_dev // pack, width)
    back = jnp.transpose(back, (0, 2, 1, 3)).reshape(total, tr_dev // pack, pack * width)
    (returned,) = swap(back, sizes, 1)
    returned = returned.reshape(total, tr_dev // pack, pack, width)
    own_mult = jnp.transpose(returned, (2, 1, 0, 3)).reshape(tr_dev, total * width)
    clean = (spectra.astype(f32) - own_mult.astype(f32)).astype(bf16)
    sums = lax.dot_general(clean, dft, (((1,), (1,)), ((), ())), preferred_element_type=f32)
    return (2.0 * sums).astype(bf16)[None]


def solution(mesh):
    n_freq, n_mid, n_off = (mesh.shape[name] for name in ("freq", "mid", "off"))

    def run(traces, time_filter, midpoint_of, offset_of, shrink_level):
        n_freqs = shrink_level.shape[0]
        n_time = traces.shape[2]
        pieces = n_freq * n_mid * n_off
        count = n_freqs // pieces
        dft = dft_table(n_time, pieces, count).reshape(n_time, n_freq, n_mid, n_off, -1)
        weights = radon_table(n_freqs)
        part_traces = traces.shape[0] * traces.shape[1] // mesh.shape["group"]
        if small(part_traces, n_off, n_mid, 2 * count):
            dft = np.ascontiguousarray(dft[: n_time // 2].transpose(2, 0, 3, 1, 4)).reshape(n_mid, n_time // 2, -1)
            inv = np.ascontiguousarray(dft.transpose(0, 2, 1)) * np.asarray(2, dft.dtype)
            weights = weights.reshape(n_freqs // 2, 2, 2 * NOFF, NP).transpose(0, 2, 1, 3)
            weights = np.ascontiguousarray(weights).reshape(n_freqs // 2, 2 * NOFF, 2 * NP)
        else:
            dft = np.ascontiguousarray(dft.transpose(0, 3, 2, 1, 4)).reshape(n_time, 2 * n_freqs)
            inv = np.zeros((1,), dft.dtype)
        return jax.shard_map(
            on_device,
            mesh=mesh,
            in_specs=(
                P(),
                P(),
                P(),
                P("off", ("group", "mid", "freq"), None),
                P(),
                P("off", "group"),
                P("off", "group"),
                P("freq"),
            ),
            out_specs=P("off", ("group", "mid", "freq"), None),
            check_vma=False,
        )(jnp.asarray(dft), jnp.asarray(inv), jnp.asarray(weights), traces, time_filter, midpoint_of, offset_of, shrink_level)

    return run
```

```python
import functools
import math

import jax
import jax.numpy as jnp
import numpy as np
from jax import lax
from jax.experimental import pallas as pl
from jax.experimental.pallas import tpu as pltpu
from jax.sharding import PartitionSpec as P

NOFF = 128
NP = 128
radon_period = 4096
VMEM = pl.BlockSpec(memory_space=pltpu.VMEM)
ANY = pl.BlockSpec(memory_space=pl.ANY)


def dft_table(n_time, n_bands, band_size):
    sample = np.arange(n_time, dtype=np.int64)[:, None]
    freq_index = np.arange(n_bands * band_size, dtype=np.int64)[None, :]
    angle = 2.0 * np.pi * (sample * freq_index % n_time) / n_time
    scale_f = 1.0 / math.sqrt(n_time)
    cosine = (np.cos(angle) * scale_f).reshape(n_time, n_bands, band_size)
    sine = (-np.sin(angle) * scale_f).reshape(n_time, n_bands, band_size)
    table = np.stack([cosine, sine], axis=2).reshape(n_time, n_bands * 2 * band_size)
    return table.astype(np.float32).astype(jnp.bfloat16)


def radon_table(n_freqs):
    freq_index = np.arange(n_freqs, dtype=np.int64)[:, None, None]
    offset_index = np.arange(NOFF, dtype=np.int64)[None, :, None]
    slowness = np.arange(NP, dtype=np.int64)[None, None, :]
    turns = freq_index * slowness % radon_period * (offset_index * offset_index % radon_period) % radon_period
    circle = 2.0 * np.pi * np.arange(radon_period) / radon_period
    scale_r = 1.0 / math.sqrt(NOFF)
    cosine = (np.cos(circle) * scale_r).astype(np.float32).astype(jnp.bfloat16)[turns]
    sine = (np.sin(circle) * scale_r).astype(np.float32).astype(jnp.bfloat16)[turns]
    return np.stack([cosine, sine], axis=1).reshape(n_freqs, 2 * NOFF, NP)


def signal(barrier, **device):
    pl.semaphore_signal(barrier, inc=1, device_id=device, device_id_type=pl.DeviceIdType.MESH)


def send(src, dst, send_sem, recv_sem, **device):
    return pltpu.make_async_remote_copy(
        src_ref=src,
        dst_ref=dst,
        send_sem=send_sem,
        recv_sem=recv_sem,
        device_id=device,
        device_id_type=pl.DeviceIdType.MESH,
    )


def place(sizes):
    names = ("off", "mid", "freq")
    here = [lax.axis_index(name) for name in names]
    index = (here[0] * sizes[1] + here[1]) * sizes[2] + here[2]
    total = sizes[0] * sizes[1] * sizes[2]

    def ahead(i):
        there = (index + i) % total
        return there, dict(off=there // (sizes[1] * sizes[2]), mid=there // sizes[2] % sizes[1], freq=there % sizes[2])

    return index, total, ahead


def swap_kernel(sizes, with_ids, *refs):
    if with_ids:
        blocks, ids, got, got_ids, own_sem, send_sem, recv_sem, id_own, id_send, id_recv = refs
    else:
        blocks, got, own_sem, send_sem, recv_sem = refs
    index, total, ahead = place(sizes)
    n_off = sizes[0]
    barrier = pltpu.get_barrier_semaphore()

    @pl.loop(1, total)
    def _(i):
        signal(barrier, **ahead(i)[1])

    own = pltpu.make_async_copy(blocks.at[index], got.at[index], own_sem)
    own.start()
    pl.semaphore_wait(barrier, total - 1)

    def block_copy(i):
        there, device = ahead(i)
        return send(blocks.at[there], got.at[index], send_sem.at[i], recv_sem.at[i], **device)

    def id_copy(d):
        off = lax.axis_index("off")
        return send(ids, got_ids.at[off], id_send.at[d], id_recv.at[d], off=(off + d) % n_off)

    if with_ids:
        own_ids = pltpu.make_async_copy(ids, got_ids.at[lax.axis_index("off")], id_own)
        own_ids.start()
        for d in range(1, n_off):
            id_copy(d).start()

    @pl.loop(1, total)
    def _(i):
        block_copy(i).start()

    own.wait()
    if with_ids:
        own_ids.wait()
        for d in range(1, n_off):
            id_copy(d).wait()

    @pl.loop(1, total)
    def _(i):
        block_copy(i).wait()


def swap(blocks, sizes, collective_id, ids=None):
    total, n_off = blocks.shape[0], sizes[0]
    dma = pltpu.SemaphoreType.DMA
    shapes = [jax.ShapeDtypeStruct(blocks.shape, blocks.dtype)]
    scratch = [dma, dma((total,)), dma((total,))]
    operands = [blocks]
    if ids is not None:
        shapes.append(jax.ShapeDtypeStruct((n_off,) + ids.shape, ids.dtype))
        scratch += [dma, dma((n_off,)), dma((n_off,))]
        operands.append(ids)
    return pl.pallas_call(
        functools.partial(swap_kernel, sizes, ids is not None),
        out_shape=shapes,
        in_specs=[VMEM] * len(operands),
        out_specs=[VMEM] * len(shapes),
        scratch_shapes=scratch,
        compiler_params=pltpu.CompilerParams(collective_id=collective_id, has_side_effects=True),
    )(*operands)


def radon_kernel(n_mid, n_off, smooth, level, table, out, weights, sem):
    count, mids = smooth.shape[1:3]
    q = (lax.axis_index("freq") * n_mid + lax.axis_index("mid")) * n_off + lax.axis_index("off")
    fetch = pltpu.make_async_copy(table.at[pl.ds(q * count, count)], weights, sem)
    fetch.start()
    re = smooth[0].astype(jnp.float32)
    im = smooth[1].astype(jnp.float32)
    first = jnp.concatenate([re, -im], axis=2)
    second = jnp.concatenate([im, re], axis=2)
    x = jnp.concatenate([first, second], axis=1).astype(jnp.bfloat16)
    fetch.wait()
    model = lax.dot_general(x, weights[...], (((2,), (1,)), ((0,), (0,))), preferred_element_type=jnp.float32)
    model_re, model_im = model[:, :mids], model[:, mids:]
    power = model_re * model_re + model_im * model_im
    keep = (lax.broadcasted_iota(jnp.int32, power.shape, 2) >= NP // 4).astype(jnp.float32)
    lev = level[...]
    factor = power / (power + lev * lev) * keep
    kept = jnp.concatenate([model_re * factor, model_im * factor], axis=1).astype(jnp.bfloat16)
    both = lax.dot_general(kept, weights[...], (((2,), (2,)), ((0,), (0,))), preferred_element_type=jnp.float32)
    out[0] = (both[:, :mids, :NOFF] + both[:, mids:, NOFF:]).astype(jnp.bfloat16)
    out[1] = (both[:, mids:, :NOFF] - both[:, :mids, NOFF:]).astype(jnp.bfloat16)


def radon(smooth, level, table, n_mid, n_off):
    count = smooth.shape[1]
    return pl.pallas_call(
        functools.partial(radon_kernel, n_mid, n_off),
        out_shape=jax.ShapeDtypeStruct(smooth.shape, jnp.bfloat16),
        in_specs=[VMEM, VMEM, ANY],
        out_specs=VMEM,
        scratch_shapes=[pltpu.VMEM((count, 2 * NOFF, NP), jnp.bfloat16), pltpu.SemaphoreType.DMA],
        compiler_params=pltpu.CompilerParams(vmem_limit_bytes=24 * 1024 * 1024),
    )(smooth, level, table)


def fused_kernel(sizes, traces_hbm, filter_hbm, mid_hbm, off_hbm, level_hbm, dft_hbm, inv_hbm, table_hbm, out, traces, filt, mid_ids, off_ids, level, dft, inv, weights, keys, key_col, near, same, blocks, got, back, ret, routes, cube, lev, load_sem, filt_sem, dft_sem, send_sem, recv_sem, id_send, id_recv):
    n_off, n_mid, n_freq = sizes
    total = n_off * n_mid * n_freq
    off, mid, freq = (lax.axis_index(name) for name in ("off", "mid", "freq"))
    f32, bf16 = jnp.float32, jnp.bfloat16
    lines, wide = blocks.shape[1:]
    width = wide // 2
    count = width // 2
    half = NOFF // n_off
    mids = lev.shape[1]
    cells = mids * half
    per_half = keys.shape[2]
    spacing = 2 * mids
    group = n_off * n_freq * width

    def peer(dm, df, do):
        m, f, o = lax.rem(mid + dm, n_mid), lax.rem(freq + df, n_freq), lax.rem(off + do, n_off)
        return (o * n_mid + m) * n_freq + f, dict(off=o, mid=m, freq=f)

    index = (off * n_mid + mid) * n_freq + freq
    far_first = sorted(range(n_mid), key=lambda dm: (dm == 0, min(dm, n_mid - dm), -dm))
    peers = [(dm, df, do) for df in reversed(range(n_freq)) for do in reversed(range(n_off)) for dm in far_first]
    others = [p for p in peers if p != (0, 0, 0)]
    barrier = pltpu.get_barrier_semaphore()
    for p in others:
        signal(barrier, **peer(*p)[1])

    def load(src, dst, sem):
        copy = pltpu.make_async_copy(src, dst, sem)
        copy.start()
        return copy

    span = filt.shape[1] // n_mid
    get_traces = load(traces_hbm, traces, load_sem.at[0])
    get_filter = [
        load(filter_hbm.at[:, pl.ds(i * span, span)], filt.at[:, pl.ds(i * span, span)], filt_sem.at[i])
        for i in range(n_mid)
    ]
    get_mid = load(mid_hbm, mid_ids, load_sem.at[1])
    get_off = load(off_hbm, off_ids, load_sem.at[2])
    get_level = load(level_hbm, level, load_sem.at[3])
    q = (freq * n_mid + mid) * n_off + off
    pairs = weights.shape[0]

    get_traces.wait()
    parts = []
    for i in range(n_mid):
        get_filter[i].wait()
        if i == 0:
            get_dft = [load(dft_hbm.at[m], dft.at[m], dft_sem.at[m]) for m in range(n_mid)]
        part = jnp.dot(traces[...], filt[:, i * span : (i + 1) * span], preferred_element_type=f32)
        parts.append(part.astype(bf16))
    folds = n_mid // 2
    stacked = jnp.concatenate([jnp.concatenate(parts[i * folds :][:folds], axis=1) for i in range(2)], axis=0)
    odd = lax.broadcasted_iota(jnp.int32, (1, group), 1) % 2 == 1
    def id_copy(d):
        return send(keys.at[off], keys.at[off], id_send.at[d], id_recv.at[d], off=lax.rem(off + d, n_off))

    def block_copy(way, src, dst, p):
        there, device = peer(*p)
        slot = (p[2] * n_freq + p[1]) * n_mid + p[0]
        return send(src.at[there], dst.at[index], send_sem.at[way, slot], recv_sem.at[way, slot], **device)

    for get in get_dft:
        get.wait()
    get_weights = load(table_hbm.at[pl.ds(q * pairs, pairs)], weights, load_sem.at[4])
    get_inv = load(inv_hbm, inv, load_sem.at[5])
    low = lax.broadcasted_iota(jnp.int32, (lines, wide), 1) < width
    for m in range(n_mid):
        halves = jnp.dot(stacked, dft[m], preferred_element_type=f32)
        first, second = halves[: 2 * lines], halves[2 * lines :]
        spectra = first + jnp.where(odd, -second, second)
        for i in range(0, n_off * n_freq, 2):
            top, bottom = (spectra[pk * lines :, i * width :][:lines, :wide] for pk in range(2))
            pair = jnp.where(low, top, pltpu.roll(bottom, width, 1)), jnp.where(low, pltpu.roll(top, width, 1), bottom)
            for at in range(2):
                o, f = (i + at) // n_freq, (i + at) % n_freq
                blocks[(o * n_mid + m) * n_freq + f] = pair[at].astype(bf16)
    get_mid.wait()
    get_off.wait()
    keys[off] = (off_ids[...] - off * half) * spacing + mid_ids[...]
    pl.semaphore_wait(barrier, total - 1)
    for d in range(1, n_off):
        id_copy(d).start()
    for p in others:
        block_copy(0, blocks, got, p).start()
    got[index] = blocks[index]

    get_level.wait()
    for k in range(count):
        own_level = level[(mid * n_off + off) * count + k]
        lev[k] = jnp.full((mids, NP), own_level * own_level, f32)
    for d in range(1, n_off):
        id_copy(d).wait_recv()

    def column_key(shape, dim, o):
        col = lax.broadcasted_iota(jnp.int32, shape, dim)
        j, u, h = col // NOFF, col // half % 2, col % half
        return (h * spacing + 2 * j + (u + o) % 2).astype(f32)

    for o in range(n_off):
        key = keys[o].astype(f32)
        n_src = total // n_off
        side = n_src // 2
        pieces = [[key[:, (s * 2 + pk) * lines :][:, :lines] for s in range(n_src)] for pk in range(2)]
        staged = [piece for g in range(2) for pk in range(2) for piece in pieces[pk][g * side : (g + 1) * side]]
        key = jnp.concatenate(staged, axis=1)
        key_col[o] = jnp.transpose(jnp.broadcast_to(key, (NOFF, per_half)))
        col_of_lane = column_key((1, cells), 1, o)
        step = 64

        @pl.loop(0, per_half // step)
        def _(j):
            here = pl.multiple_of(j * step, step)
            own = key_col[o, pl.ds(here, step)]
            own = jnp.concatenate([own] * (cells // NOFF), axis=1)
            away = jnp.abs(own - col_of_lane)
            near[o, pl.ds(here, step)] = jnp.where(away == 0, 0.5, jnp.where(away == 1, 0.25, 0.0)).astype(bf16)

        @pl.loop(0, cells // step)
        def _(j):
            here = pl.multiple_of(j * step, step)
            col = lax.broadcasted_iota(jnp.int32, (step, NOFF), 0) + here
            c, u, h = col // NOFF, col // half % 2, col % half
            col = (h * spacing + 2 * c + (u + o) % 2).astype(f32)
            col = jnp.concatenate([col] * (per_half // NOFF), axis=1)
            same[o, pl.ds(here, step)] = jnp.where(col == key, 1.0, 0.0).astype(bf16)

    get_weights.wait()
    n_src = total // n_off
    side, reach = n_src // 2, n_mid // 2
    near_side = mid // reach
    gathered = [None] * n_off
    for step, g in enumerate((near_side, 1 - near_side)):
        for j in range(reach):
            m = g * reach + (lax.rem(mid + j, reach) if step == 0 else j)
            dm = 0 if step == 0 and j == 0 else lax.rem(mid - m + n_mid, n_mid)
            for df in range(n_freq):
                for do in range(n_off):
                    if step or j or df or do:
                        block_copy(0, blocks, got, (dm, df, do)).wait_recv()
        for o in range(n_off):
            rows = got[pl.ds(o * n_src + g * side, side)].reshape(side * lines, wide)
            rows = jnp.transpose(rows.astype(f32)).astype(bf16)
            rows = jnp.concatenate([rows[:width], rows[width:]], axis=1)
            spot = pl.multiple_of(g * (per_half // 2), per_half // 2)
            part = jnp.dot(rows, near[o, pl.ds(spot, per_half // 2)], preferred_element_type=f32)
            gathered[o] = part if step == 0 else gathered[o] + part
    low = lax.broadcasted_iota(jnp.int32, (width, NOFF), 1) < half
    for j in range(mids // 2):
        a, b = (g[:, j * NOFF : (j + 1) * NOFF] for g in gathered)
        cube[pl.ds(2 * j, width, stride=mids), :] = jnp.where(low, a, b)
        cube[pl.ds(2 * j + 1, width, stride=mids), :] = pltpu.roll(jnp.where(low, b, a), half, 1)
    re, im = cube[...].reshape(2, count, mids, NOFF)
    first = jnp.concatenate([re, -im], axis=2)
    second = jnp.concatenate([im, re], axis=2)
    x = jnp.concatenate([first, second], axis=1).astype(bf16).reshape(pairs, 4 * mids, 2 * NOFF)
    both = lax.dot_general(x, weights[...], (((2,), (1,)), ((0,), (0,))), preferred_element_type=f32)
    keep = (lax.broadcasted_iota(jnp.int32, (mids, NP), 1) >= NP // 4).astype(f32)
    levels = lev[...].reshape(pairs, 2, mids, NP)
    kept = []
    for i in range(2):
        model_re = both[:, 2 * i * mids : (2 * i + 1) * mids, i * NP : (i + 1) * NP]
        model_im = both[:, (2 * i + 1) * mids : (2 * i + 2) * mids, i * NP : (i + 1) * NP]
        power = model_re * model_re + model_im * model_im
        factor = power / (power + levels[:, i]) * keep
        part = jnp.concatenate([model_re * factor, model_im * factor], axis=1)
        blank = jnp.zeros_like(part)
        kept.append(jnp.concatenate([blank] * i + [part] + [blank] * (1 - i), axis=2))
    kept = jnp.concatenate(kept, axis=1).astype(bf16)
    both = lax.dot_general(kept, weights[...], (((2,), (2,)), ((0,), (0,))), preferred_element_type=f32)
    both = both.reshape(count, 2 * mids, 2 * NOFF)
    mult_re = both[:, :mids, :NOFF] + both[:, mids:, NOFF:]
    mult_im = both[:, mids:, :NOFF] - both[:, :mids, NOFF:]
    cube[...] = jnp.concatenate([mult_re, mult_im], axis=0).reshape(width * mids, NOFF)
    mult = [[], []]
    for j in range(mids // 2):
        even = cube[pl.ds(2 * j, width, stride=mids), :]
        other = pltpu.roll(cube[pl.ds(2 * j + 1, width, stride=mids), :], half, 1)
        mult[0].append(jnp.where(low, even, other))
        mult[1].append(jnp.where(low, other, even))
    for o in range(n_off):
        routes[o] = jnp.concatenate(mult[o], axis=1).astype(bf16)
    for step, g in enumerate((1 - near_side, near_side)):
        spot = pl.multiple_of(g * (per_half // 2), per_half // 2)
        for o in range(n_off):
            routed = jnp.dot(routes[o], same[o, :, pl.ds(spot, per_half // 2)], preferred_element_type=f32)
            routed = jnp.concatenate([routed[:, : per_half // 4], routed[:, per_half // 4 :]], axis=0)
            back[pl.ds(o * n_src + g * side, side)] = jnp.transpose(routed).astype(bf16).reshape(side, lines, wide)
        for j in range(reach):
            for do in range(n_off):
                for df in reversed(range(n_freq)):
                    m = g * reach + (j if step == 0 else lax.rem(mid + j, reach))
                    dm = 0 if step and j == 0 else lax.rem(m - mid + n_mid, n_mid)
                    if step == 0 or j or df or do:
                        block_copy(1, back, ret, (dm, df, do)).start()
    ret[index] = back[index]
    for p in others:
        block_copy(0, blocks, got, p).wait_send()
    for d in range(1, n_off):
        id_copy(d).wait_send()

    get_inv.wait()
    low = lax.broadcasted_iota(jnp.int32, (lines, wide), 1) < width
    total_out = None
    for dm in reversed(far_first):
        m = lax.rem(mid + dm, n_mid)
        if dm == far_first[0]:
            for p in others:
                block_copy(1, back, ret, p).wait_send()
        for p in others:
            if (p[0] + dm) % n_mid == 0:
                block_copy(1, back, ret, p).wait_recv()
        clean = []
        for o in range(n_off):
            for f in range(n_freq):
                d = (o * n_mid + m) * n_freq + f
                clean.append(blocks[d].astype(f32) - ret[d].astype(f32))
        top, bottom = [], []
        for i in range(0, len(clean), 2):
            top.append(jnp.where(low, clean[i], pltpu.roll(clean[i + 1], width, 1)))
            bottom.append(jnp.where(low, pltpu.roll(clean[i], width, 1), clean[i + 1]))
        clean = jnp.concatenate([jnp.concatenate(top, axis=1), jnp.concatenate(bottom, axis=1)], axis=0)
        clean = jnp.concatenate([clean, jnp.where(odd, -clean, clean)], axis=0).astype(bf16)
        sums = jnp.dot(clean, inv[m], preferred_element_type=f32)
        total_out = sums if total_out is None else total_out + sums
    n_time = inv.shape[2]
    out[:, :n_time] = total_out[: 2 * lines].astype(bf16)
    out[:, n_time:] = total_out[2 * lines :].astype(bf16)


def fused(traces, time_filter, midpoint_of, offset_of, level, dft, inv, table, sizes):
    n_off, n_mid, n_freq = sizes
    total = n_off * n_mid * n_freq
    count = level.shape[0] // (n_mid * n_off)
    width = 2 * count
    lines = traces.shape[0] // 2
    per_half = midpoint_of.shape[1]
    mids = n_off * per_half // NOFF
    cells = per_half
    dma = pltpu.SemaphoreType.DMA
    f32, bf16, i32 = jnp.float32, jnp.bfloat16, jnp.int32
    shape = (total, lines, 2 * width)
    hbm = pl.BlockSpec(memory_space=pltpu.HBM)
    operands = (traces, time_filter, midpoint_of, offset_of, level, dft, inv, table)
    return pl.pallas_call(
        functools.partial(fused_kernel, sizes),
        out_shape=jax.ShapeDtypeStruct(traces.shape, traces.dtype),
        in_specs=[hbm] * 8,
        out_specs=VMEM,
        scratch_shapes=[
            pltpu.VMEM(traces.shape, bf16),
            pltpu.VMEM(time_filter.shape, bf16),
            pltpu.VMEM(midpoint_of.shape, i32),
            pltpu.VMEM(offset_of.shape, i32),
            pltpu.SMEM(level.shape, f32),
            pltpu.VMEM(dft.shape, bf16),
            pltpu.VMEM(inv.shape, bf16),
            pltpu.VMEM((count // 2,) + table.shape[1:], bf16),
            pltpu.VMEM((n_off, 1, per_half), i32),
            pltpu.VMEM((n_off, per_half, NOFF), f32),
            pltpu.VMEM((n_off, per_half, cells), bf16),
            pltpu.VMEM((n_off, cells, per_half), bf16),
            pltpu.VMEM(shape, bf16),
            pltpu.VMEM(shape, bf16),
            pltpu.VMEM(shape, bf16),
            pltpu.VMEM(shape, bf16),
            pltpu.VMEM((n_off, width, cells), bf16),
            pltpu.VMEM((width * mids, NOFF), f32),
            pltpu.VMEM((count, mids, NP), f32),
            dma((6,)),
            dma((n_mid,)),
            dma((n_mid,)),
            dma((2, total)),
            dma((2, total)),
            dma((n_off,)),
            dma((n_off,)),
        ],
        compiler_params=pltpu.CompilerParams(
            collective_id=2, has_side_effects=True, vmem_limit_bytes=32 * 1024 * 1024
        ),
    )(*(pltpu.with_memory_space_constraint(x, pltpu.HBM) for x in operands))


def small(n_traces, n_off, n_mid, width):
    return n_traces <= 4096 and n_off == 2 and n_mid % 2 == 0 and width == 64


def on_device(dft, inv, weights, traces, time_filter, midpoint_of, offset_of, shrink_level):
    n_mid = lax.axis_size("mid")
    n_freq = lax.axis_size("freq")
    n_off = lax.axis_size("off")
    sizes = (n_off, n_mid, n_freq)
    total = n_off * n_mid * n_freq
    me_mid = lax.axis_index("mid")
    me_off = lax.axis_index("off")
    tr_dev = traces.shape[1]
    count = shrink_level.shape[0] // (n_mid * n_off)
    width = 2 * count
    pack = max(1, min(tr_dev, 128 // width))
    n_traces = total * tr_dev
    n_mids = n_traces // NOFF
    f32, bf16 = jnp.float32, jnp.bfloat16

    if small(n_traces, n_off, n_mid, width):
        return fused(traces[0], time_filter, midpoint_of, offset_of, shrink_level, dft, inv, weights, sizes)[None]
    own_ids = midpoint_of * NOFF + offset_of
    filtered = jnp.dot(traces[0], time_filter, preferred_element_type=f32).astype(bf16)
    spectra = jnp.dot(filtered, dft, preferred_element_type=f32).astype(bf16)
    blocks = spectra.reshape(pack, tr_dev // pack, total, width)
    blocks = jnp.transpose(blocks, (2, 1, 0, 3)).reshape(total, tr_dev // pack, pack * width)
    own_levels = lax.dynamic_slice_in_dim(shrink_level, (me_mid * n_off + me_off) * count, count)
    level = jnp.broadcast_to(own_levels[:, None, None], (count, 1, NP))
    rows, ids = swap(blocks, sizes, 0, own_ids)
    rows = rows.reshape(total, tr_dev // pack, pack, width)
    rows = jnp.transpose(rows, (0, 2, 1, 3)).reshape(n_traces, width)
    cell_of = ids.reshape(n_traces)
    gather = jnp.zeros((n_traces, width), bf16).at[cell_of].set(rows)
    edged = jnp.pad(gather.reshape(n_mids, NOFF, 2, count).astype(f32), ((1, 1), (0, 0), (0, 0), (0, 0)))
    smooth = ((edged[:-2] + 2.0 * edged[1:-1] + edged[2:]) * 0.25).astype(bf16)
    smooth = jnp.transpose(smooth, (2, 3, 0, 1))
    mult = radon(smooth, level, weights, n_mid, n_off).reshape(width, n_traces)
    back = jnp.transpose(mult)[cell_of].reshape(total, pack, tr_dev // pack, width)
    back = jnp.transpose(back, (0, 2, 1, 3)).reshape(total, tr_dev // pack, pack * width)
    (returned,) = swap(back, sizes, 1)
    returned = returned.reshape(total, tr_dev // pack, pack, width)
    own_mult = jnp.transpose(returned, (2, 1, 0, 3)).reshape(tr_dev, total * width)
    clean = (spectra.astype(f32) - own_mult.astype(f32)).astype(bf16)
    sums = lax.dot_general(clean, dft, (((1,), (1,)), ((), ())), preferred_element_type=f32)
    return (2.0 * sums).astype(bf16)[None]


def solution(mesh):
    n_freq, n_mid, n_off = (mesh.shape[name] for name in ("freq", "mid", "off"))

    def run(traces, time_filter, midpoint_of, offset_of, shrink_level):
        n_freqs = shrink_level.shape[0]
        n_time = traces.shape[2]
        pieces = n_freq * n_mid * n_off
        count = n_freqs // pieces
        dft = dft_table(n_time, pieces, count).reshape(n_time, n_freq, n_mid, n_off, -1)
        weights = radon_table(n_freqs)
        part_traces = traces.shape[0] * traces.shape[1] // mesh.shape["group"]
        if small(part_traces, n_off, n_mid, 2 * count):
            dft = np.ascontiguousarray(dft[: n_time // 2].transpose(2, 0, 3, 1, 4)).reshape(n_mid, n_time // 2, -1)
            inv = np.ascontiguousarray(dft.transpose(0, 2, 1)) * np.asarray(2, dft.dtype)
            weights = weights.reshape(n_freqs // 2, 2, 2 * NOFF, NP).transpose(0, 2, 1, 3)
            weights = np.ascontiguousarray(weights).reshape(n_freqs // 2, 2 * NOFF, 2 * NP)
        else:
            dft = np.ascontiguousarray(dft.transpose(0, 3, 2, 1, 4)).reshape(n_time, 2 * n_freqs)
            inv = np.zeros((1,), dft.dtype)
        return jax.shard_map(
            on_device,
            mesh=mesh,
            in_specs=(
                P(),
                P(),
                P(),
                P("off", ("group", "mid", "freq"), None),
                P(),
                P("off", "group"),
                P("off", "group"),
                P("freq"),
            ),
            out_specs=P("off", ("group", "mid", "freq"), None),
            check_vma=False,
        )(jnp.asarray(dft), jnp.asarray(inv), jnp.asarray(weights), traces, time_filter, midpoint_of, offset_of, shrink_level)

    return run
```

```python
import functools
import math

import jax
import jax.numpy as jnp
import numpy as np
from jax import lax
from jax.experimental import pallas as pl
from jax.experimental.pallas import tpu as pltpu
from jax.sharding import PartitionSpec as P

NOFF = 128
NP = 128
radon_period = 4096
VMEM = pl.BlockSpec(memory_space=pltpu.VMEM)
ANY = pl.BlockSpec(memory_space=pl.ANY)


def dft_table(n_time, n_bands, band_size):
    sample = np.arange(n_time, dtype=np.int64)[:, None]
    freq_index = np.arange(n_bands * band_size, dtype=np.int64)[None, :]
    angle = 2.0 * np.pi * (sample * freq_index % n_time) / n_time
    scale_f = 1.0 / math.sqrt(n_time)
    cosine = (np.cos(angle) * scale_f).reshape(n_time, n_bands, band_size)
    sine = (-np.sin(angle) * scale_f).reshape(n_time, n_bands, band_size)
    table = np.stack([cosine, sine], axis=2).reshape(n_time, n_bands * 2 * band_size)
    return table.astype(np.float32).astype(jnp.bfloat16)


def radon_table(n_freqs):
    freq_index = np.arange(n_freqs, dtype=np.int64)[:, None, None]
    offset_index = np.arange(NOFF, dtype=np.int64)[None, :, None]
    slowness = np.arange(NP, dtype=np.int64)[None, None, :]
    turns = freq_index * slowness % radon_period * (offset_index * offset_index % radon_period) % radon_period
    circle = 2.0 * np.pi * np.arange(radon_period) / radon_period
    scale_r = 1.0 / math.sqrt(NOFF)
    cosine = (np.cos(circle) * scale_r).astype(np.float32).astype(jnp.bfloat16)[turns]
    sine = (np.sin(circle) * scale_r).astype(np.float32).astype(jnp.bfloat16)[turns]
    return np.stack([cosine, sine], axis=1).reshape(n_freqs, 2 * NOFF, NP)


def signal(barrier, **device):
    pl.semaphore_signal(barrier, inc=1, device_id=device, device_id_type=pl.DeviceIdType.MESH)


def send(src, dst, send_sem, recv_sem, **device):
    return pltpu.make_async_remote_copy(
        src_ref=src,
        dst_ref=dst,
        send_sem=send_sem,
        recv_sem=recv_sem,
        device_id=device,
        device_id_type=pl.DeviceIdType.MESH,
    )


def place(sizes):
    names = ("off", "mid", "freq")
    here = [lax.axis_index(name) for name in names]
    index = (here[0] * sizes[1] + here[1]) * sizes[2] + here[2]
    total = sizes[0] * sizes[1] * sizes[2]

    def ahead(i):
        there = (index + i) % total
        return there, dict(off=there // (sizes[1] * sizes[2]), mid=there // sizes[2] % sizes[1], freq=there % sizes[2])

    return index, total, ahead


def swap_kernel(sizes, with_ids, *refs):
    if with_ids:
        blocks, ids, got, got_ids, own_sem, send_sem, recv_sem, id_own, id_send, id_recv = refs
    else:
        blocks, got, own_sem, send_sem, recv_sem = refs
    index, total, ahead = place(sizes)
    n_off = sizes[0]
    barrier = pltpu.get_barrier_semaphore()

    @pl.loop(1, total)
    def _(i):
        signal(barrier, **ahead(i)[1])

    own = pltpu.make_async_copy(blocks.at[index], got.at[index], own_sem)
    own.start()
    pl.semaphore_wait(barrier, total - 1)

    def block_copy(i):
        there, device = ahead(i)
        return send(blocks.at[there], got.at[index], send_sem.at[i], recv_sem.at[i], **device)

    def id_copy(d):
        off = lax.axis_index("off")
        return send(ids, got_ids.at[off], id_send.at[d], id_recv.at[d], off=(off + d) % n_off)

    if with_ids:
        own_ids = pltpu.make_async_copy(ids, got_ids.at[lax.axis_index("off")], id_own)
        own_ids.start()
        for d in range(1, n_off):
            id_copy(d).start()

    @pl.loop(1, total)
    def _(i):
        block_copy(i).start()

    own.wait()
    if with_ids:
        own_ids.wait()
        for d in range(1, n_off):
            id_copy(d).wait()

    @pl.loop(1, total)
    def _(i):
        block_copy(i).wait()


def swap(blocks, sizes, collective_id, ids=None):
    total, n_off = blocks.shape[0], sizes[0]
    dma = pltpu.SemaphoreType.DMA
    shapes = [jax.ShapeDtypeStruct(blocks.shape, blocks.dtype)]
    scratch = [dma, dma((total,)), dma((total,))]
    operands = [blocks]
    if ids is not None:
        shapes.append(jax.ShapeDtypeStruct((n_off,) + ids.shape, ids.dtype))
        scratch += [dma, dma((n_off,)), dma((n_off,))]
        operands.append(ids)
    return pl.pallas_call(
        functools.partial(swap_kernel, sizes, ids is not None),
        out_shape=shapes,
        in_specs=[VMEM] * len(operands),
        out_specs=[VMEM] * len(shapes),
        scratch_shapes=scratch,
        compiler_params=pltpu.CompilerParams(collective_id=collective_id, has_side_effects=True),
    )(*operands)


def radon_kernel(n_mid, n_off, smooth, level, table, out, weights, sem):
    count, mids = smooth.shape[1:3]
    q = (lax.axis_index("freq") * n_mid + lax.axis_index("mid")) * n_off + lax.axis_index("off")
    fetch = pltpu.make_async_copy(table.at[pl.ds(q * count, count)], weights, sem)
    fetch.start()
    re = smooth[0].astype(jnp.float32)
    im = smooth[1].astype(jnp.float32)
    first = jnp.concatenate([re, -im], axis=2)
    second = jnp.concatenate([im, re], axis=2)
    x = jnp.concatenate([first, second], axis=1).astype(jnp.bfloat16)
    fetch.wait()
    model = lax.dot_general(x, weights[...], (((2,), (1,)), ((0,), (0,))), preferred_element_type=jnp.float32)
    model_re, model_im = model[:, :mids], model[:, mids:]
    power = model_re * model_re + model_im * model_im
    keep = (lax.broadcasted_iota(jnp.int32, power.shape, 2) >= NP // 4).astype(jnp.float32)
    lev = level[...]
    factor = power / (power + lev * lev) * keep
    kept = jnp.concatenate([model_re * factor, model_im * factor], axis=1).astype(jnp.bfloat16)
    both = lax.dot_general(kept, weights[...], (((2,), (2,)), ((0,), (0,))), preferred_element_type=jnp.float32)
    out[0] = (both[:, :mids, :NOFF] + both[:, mids:, NOFF:]).astype(jnp.bfloat16)
    out[1] = (both[:, mids:, :NOFF] - both[:, :mids, NOFF:]).astype(jnp.bfloat16)


def radon(smooth, level, table, n_mid, n_off):
    count = smooth.shape[1]
    return pl.pallas_call(
        functools.partial(radon_kernel, n_mid, n_off),
        out_shape=jax.ShapeDtypeStruct(smooth.shape, jnp.bfloat16),
        in_specs=[VMEM, VMEM, ANY],
        out_specs=VMEM,
        scratch_shapes=[pltpu.VMEM((count, 2 * NOFF, NP), jnp.bfloat16), pltpu.SemaphoreType.DMA],
        compiler_params=pltpu.CompilerParams(vmem_limit_bytes=24 * 1024 * 1024),
    )(smooth, level, table)


def fused_kernel(sizes, traces_hbm, filter_hbm, mid_hbm, off_hbm, level_hbm, dft_hbm, inv_hbm, table_hbm, out, traces, filt, mid_ids, off_ids, level, dft, inv, weights, keys, key_col, near, same, blocks, got, back, ret, routes, cube, lev, load_sem, filt_sem, dft_sem, send_sem, recv_sem, id_send, id_recv):
    n_off, n_mid, n_freq = sizes
    total = n_off * n_mid * n_freq
    off, mid, freq = (lax.axis_index(name) for name in ("off", "mid", "freq"))
    f32, bf16 = jnp.float32, jnp.bfloat16
    lines, wide = blocks.shape[1:]
    width = wide // 2
    count = width // 2
    half = NOFF // n_off
    mids = lev.shape[1]
    cells = mids * half
    per_half = keys.shape[2]
    spacing = 2 * mids
    group = n_off * n_freq * width

    def peer(dm, df, do):
        m, f, o = lax.rem(mid + dm, n_mid), lax.rem(freq + df, n_freq), lax.rem(off + do, n_off)
        return (o * n_mid + m) * n_freq + f, dict(off=o, mid=m, freq=f)

    index = (off * n_mid + mid) * n_freq + freq
    far_first = sorted(range(n_mid), key=lambda dm: (dm == 0, min(dm, n_mid - dm), -dm))
    peers = [(dm, df, do) for do in reversed(range(n_off)) for df in reversed(range(n_freq)) for dm in far_first]
    others = [p for p in peers if p != (0, 0, 0)]
    barrier = pltpu.get_barrier_semaphore()
    for p in others:
        signal(barrier, **peer(*p)[1])

    def load(src, dst, sem):
        copy = pltpu.make_async_copy(src, dst, sem)
        copy.start()
        return copy

    span = filt.shape[1] // n_mid
    get_traces = load(traces_hbm, traces, load_sem.at[0])
    get_filter = [
        load(filter_hbm.at[:, pl.ds(i * span, span)], filt.at[:, pl.ds(i * span, span)], filt_sem.at[i])
        for i in range(n_mid)
    ]
    get_mid = load(mid_hbm, mid_ids, load_sem.at[1])
    get_off = load(off_hbm, off_ids, load_sem.at[2])
    get_level = load(level_hbm, level, load_sem.at[3])
    q = (freq * n_mid + mid) * n_off + off
    pairs = weights.shape[0]

    get_traces.wait()
    parts = []
    for i in range(n_mid):
        get_filter[i].wait()
        if i == 0:
            get_dft = [load(dft_hbm.at[m], dft.at[m], dft_sem.at[m]) for m in range(n_mid)]
        part = jnp.dot(traces[...], filt[:, i * span : (i + 1) * span], preferred_element_type=f32)
        parts.append(part.astype(bf16))
    folds = n_mid // 2
    stacked = jnp.concatenate([jnp.concatenate(parts[i * folds :][:folds], axis=1) for i in range(2)], axis=0)
    odd = lax.broadcasted_iota(jnp.int32, (1, group), 1) % 2 == 1
    def id_copy(d):
        return send(keys.at[off], keys.at[off], id_send.at[d], id_recv.at[d], off=lax.rem(off + d, n_off))

    def block_copy(way, src, dst, p):
        there, device = peer(*p)
        slot = (p[2] * n_freq + p[1]) * n_mid + p[0]
        return send(src.at[there], dst.at[index], send_sem.at[way, slot], recv_sem.at[way, slot], **device)

    for get in get_dft:
        get.wait()
    get_weights = load(table_hbm.at[pl.ds(q * pairs, pairs)], weights, load_sem.at[4])
    get_inv = load(inv_hbm, inv, load_sem.at[5])
    low = lax.broadcasted_iota(jnp.int32, (lines, wide), 1) < width
    for m in range(n_mid):
        halves = jnp.dot(stacked, dft[m], preferred_element_type=f32)
        first, second = halves[: 2 * lines], halves[2 * lines :]
        spectra = first + jnp.where(odd, -second, second)
        for i in range(0, n_off * n_freq, 2):
            top, bottom = (spectra[pk * lines :, i * width :][:lines, :wide] for pk in range(2))
            pair = jnp.where(low, top, pltpu.roll(bottom, width, 1)), jnp.where(low, pltpu.roll(top, width, 1), bottom)
            for at in range(2):
                o, f = (i + at) // n_freq, (i + at) % n_freq
                blocks[(o * n_mid + m) * n_freq + f] = pair[at].astype(bf16)
    get_mid.wait()
    get_off.wait()
    keys[off] = (off_ids[...] - off * half) * spacing + mid_ids[...]
    pl.semaphore_wait(barrier, total - 1)
    for d in range(1, n_off):
        id_copy(d).start()
    for p in others:
        block_copy(0, blocks, got, p).start()
    got[index] = blocks[index]

    get_level.wait()
    for k in range(count):
        own_level = level[(mid * n_off + off) * count + k]
        lev[k] = jnp.full((mids, NP), own_level * own_level, f32)
    for d in range(1, n_off):
        id_copy(d).wait_recv()

    def column_key(shape, dim, o):
        col = lax.broadcasted_iota(jnp.int32, shape, dim)
        j, u, h = col // NOFF, col // half % 2, col % half
        return (h * spacing + 2 * j + (u + o) % 2).astype(f32)

    for o in range(n_off):
        key = keys[o].astype(f32)
        n_src = total // n_off
        side = n_src // 2
        pieces = [[key[:, (s * 2 + pk) * lines :][:, :lines] for s in range(n_src)] for pk in range(2)]
        staged = [piece for g in range(2) for pk in range(2) for piece in pieces[pk][g * side : (g + 1) * side]]
        key = jnp.concatenate(staged, axis=1)
        key_col[o] = jnp.transpose(jnp.broadcast_to(key, (NOFF, per_half)))
        col_of_lane = column_key((1, cells), 1, o)
        step = 64

        @pl.loop(0, per_half // step)
        def _(j):
            here = pl.multiple_of(j * step, step)
            own = key_col[o, pl.ds(here, step)]
            own = jnp.concatenate([own] * (cells // NOFF), axis=1)
            away = jnp.abs(own - col_of_lane)
            near[o, pl.ds(here, step)] = jnp.where(away == 0, 0.5, jnp.where(away == 1, 0.25, 0.0)).astype(bf16)

        @pl.loop(0, cells // step)
        def _(j):
            here = pl.multiple_of(j * step, step)
            col = lax.broadcasted_iota(jnp.int32, (step, NOFF), 0) + here
            c, u, h = col // NOFF, col // half % 2, col % half
            col = (h * spacing + 2 * c + (u + o) % 2).astype(f32)
            col = jnp.concatenate([col] * (per_half // NOFF), axis=1)
            same[o, pl.ds(here, step)] = jnp.where(col == key, 1.0, 0.0).astype(bf16)

    get_weights.wait()
    n_src = total // n_off
    side, reach = n_src // 2, n_mid // 2
    near_side = mid // reach
    gathered = [None] * n_off
    for step, g in enumerate((near_side, 1 - near_side)):
        for j in range(reach):
            m = g * reach + (lax.rem(mid + j, reach) if step == 0 else j)
            dm = 0 if step == 0 and j == 0 else lax.rem(mid - m + n_mid, n_mid)
            for df in range(n_freq):
                for do in range(n_off):
                    if step or j or df or do:
                        block_copy(0, blocks, got, (dm, df, do)).wait_recv()
        for o in range(n_off):
            rows = got[pl.ds(o * n_src + g * side, side)].reshape(side * lines, wide)
            rows = jnp.transpose(rows.astype(f32)).astype(bf16)
            rows = jnp.concatenate([rows[:width], rows[width:]], axis=1)
            spot = pl.multiple_of(g * (per_half // 2), per_half // 2)
            part = jnp.dot(rows, near[o, pl.ds(spot, per_half // 2)], preferred_element_type=f32)
            gathered[o] = part if step == 0 else gathered[o] + part
    low = lax.broadcasted_iota(jnp.int32, (width, NOFF), 1) < half
    for j in range(mids // 2):
        a, b = (g[:, j * NOFF : (j + 1) * NOFF] for g in gathered)
        cube[pl.ds(2 * j, width, stride=mids), :] = jnp.where(low, a, b)
        cube[pl.ds(2 * j + 1, width, stride=mids), :] = pltpu.roll(jnp.where(low, b, a), half, 1)
    re, im = cube[...].reshape(2, count, mids, NOFF)
    first = jnp.concatenate([re, -im], axis=2)
    second = jnp.concatenate([im, re], axis=2)
    x = jnp.concatenate([first, second], axis=1).astype(bf16).reshape(pairs, 4 * mids, 2 * NOFF)
    both = lax.dot_general(x, weights[...], (((2,), (1,)), ((0,), (0,))), preferred_element_type=f32)
    keep = (lax.broadcasted_iota(jnp.int32, (mids, NP), 1) >= NP // 4).astype(f32)
    levels = lev[...].reshape(pairs, 2, mids, NP)
    kept = []
    for i in range(2):
        model_re = both[:, 2 * i * mids : (2 * i + 1) * mids, i * NP : (i + 1) * NP]
        model_im = both[:, (2 * i + 1) * mids : (2 * i + 2) * mids, i * NP : (i + 1) * NP]
        power = model_re * model_re + model_im * model_im
        factor = power / (power + levels[:, i]) * keep
        part = jnp.concatenate([model_re * factor, model_im * factor], axis=1)
        blank = jnp.zeros_like(part)
        kept.append(jnp.concatenate([blank] * i + [part] + [blank] * (1 - i), axis=2))
    kept = jnp.concatenate(kept, axis=1).astype(bf16)
    both = lax.dot_general(kept, weights[...], (((2,), (2,)), ((0,), (0,))), preferred_element_type=f32)
    both = both.reshape(count, 2 * mids, 2 * NOFF)
    mult_re = both[:, :mids, :NOFF] + both[:, mids:, NOFF:]
    mult_im = both[:, mids:, :NOFF] - both[:, :mids, NOFF:]
    cube[...] = jnp.concatenate([mult_re, mult_im], axis=0).reshape(width * mids, NOFF)
    mult = [[], []]
    for j in range(mids // 2):
        even = cube[pl.ds(2 * j, width, stride=mids), :]
        other = pltpu.roll(cube[pl.ds(2 * j + 1, width, stride=mids), :], half, 1)
        mult[0].append(jnp.where(low, even, other))
        mult[1].append(jnp.where(low, other, even))
    for o in range(n_off):
        routes[o] = jnp.concatenate(mult[o], axis=1).astype(bf16)
    for step, g in enumerate((1 - near_side, near_side)):
        spot = pl.multiple_of(g * (per_half // 2), per_half // 2)
        for do in range(n_off):
            o = lax.rem(off + do, n_off)
            routed = jnp.dot(routes[o], same[o, :, pl.ds(spot, per_half // 2)], preferred_element_type=f32)
            routed = jnp.concatenate([routed[:, : per_half // 4], routed[:, per_half // 4 :]], axis=0)
            back[pl.ds(o * n_src + g * side, side)] = jnp.transpose(routed).astype(bf16).reshape(side, lines, wide)
            for j in range(reach):
                for df in reversed(range(n_freq)):
                    m = g * reach + (j if step == 0 else lax.rem(mid + j, reach))
                    dm = 0 if step and j == 0 else lax.rem(m - mid + n_mid, n_mid)
                    if step == 0 or j or df or do:
                        block_copy(1, back, ret, (dm, df, do)).start()
    ret[index] = back[index]
    for p in others:
        block_copy(0, blocks, got, p).wait_send()
    for d in range(1, n_off):
        id_copy(d).wait_send()

    get_inv.wait()
    low = lax.broadcasted_iota(jnp.int32, (lines, wide), 1) < width
    total_out = None
    for dm in reversed(far_first):
        m = lax.rem(mid + dm, n_mid)
        if dm == far_first[0]:
            for p in others:
                block_copy(1, back, ret, p).wait_send()
        for p in others:
            if (p[0] + dm) % n_mid == 0:
                block_copy(1, back, ret, p).wait_recv()
        clean = []
        for o in range(n_off):
            for f in range(n_freq):
                d = (o * n_mid + m) * n_freq + f
                clean.append(blocks[d].astype(f32) - ret[d].astype(f32))
        top, bottom = [], []
        for i in range(0, len(clean), 2):
            top.append(jnp.where(low, clean[i], pltpu.roll(clean[i + 1], width, 1)))
            bottom.append(jnp.where(low, pltpu.roll(clean[i], width, 1), clean[i + 1]))
        clean = jnp.concatenate([jnp.concatenate(top, axis=1), jnp.concatenate(bottom, axis=1)], axis=0)
        clean = jnp.concatenate([clean, jnp.where(odd, -clean, clean)], axis=0).astype(bf16)
        sums = jnp.dot(clean, inv[m], preferred_element_type=f32)
        total_out = sums if total_out is None else total_out + sums
    n_time = inv.shape[2]
    out[:, :n_time] = total_out[: 2 * lines].astype(bf16)
    out[:, n_time:] = total_out[2 * lines :].astype(bf16)


def fused(traces, time_filter, midpoint_of, offset_of, level, dft, inv, table, sizes):
    n_off, n_mid, n_freq = sizes
    total = n_off * n_mid * n_freq
    count = level.shape[0] // (n_mid * n_off)
    width = 2 * count
    lines = traces.shape[0] // 2
    per_half = midpoint_of.shape[1]
    mids = n_off * per_half // NOFF
    cells = per_half
    dma = pltpu.SemaphoreType.DMA
    f32, bf16, i32 = jnp.float32, jnp.bfloat16, jnp.int32
    shape = (total, lines, 2 * width)
    hbm = pl.BlockSpec(memory_space=pltpu.HBM)
    operands = (traces, time_filter, midpoint_of, offset_of, level, dft, inv, table)
    return pl.pallas_call(
        functools.partial(fused_kernel, sizes),
        out_shape=jax.ShapeDtypeStruct(traces.shape, traces.dtype),
        in_specs=[hbm] * 8,
        out_specs=VMEM,
        scratch_shapes=[
            pltpu.VMEM(traces.shape, bf16),
            pltpu.VMEM(time_filter.shape, bf16),
            pltpu.VMEM(midpoint_of.shape, i32),
            pltpu.VMEM(offset_of.shape, i32),
            pltpu.SMEM(level.shape, f32),
            pltpu.VMEM(dft.shape, bf16),
            pltpu.VMEM(inv.shape, bf16),
            pltpu.VMEM((count // 2,) + table.shape[1:], bf16),
            pltpu.VMEM((n_off, 1, per_half), i32),
            pltpu.VMEM((n_off, per_half, NOFF), f32),
            pltpu.VMEM((n_off, per_half, cells), bf16),
            pltpu.VMEM((n_off, cells, per_half), bf16),
            pltpu.VMEM(shape, bf16),
            pltpu.VMEM(shape, bf16),
            pltpu.VMEM(shape, bf16),
            pltpu.VMEM(shape, bf16),
            pltpu.VMEM((n_off, width, cells), bf16),
            pltpu.VMEM((width * mids, NOFF), f32),
            pltpu.VMEM((count, mids, NP), f32),
            dma((6,)),
            dma((n_mid,)),
            dma((n_mid,)),
            dma((2, total)),
            dma((2, total)),
            dma((n_off,)),
            dma((n_off,)),
        ],
        compiler_params=pltpu.CompilerParams(
            collective_id=2, has_side_effects=True, vmem_limit_bytes=32 * 1024 * 1024
        ),
    )(*(pltpu.with_memory_space_constraint(x, pltpu.HBM) for x in operands))


def small(n_traces, n_off, n_mid, width):
    return n_traces <= 4096 and n_off == 2 and n_mid % 2 == 0 and width == 64


def on_device(dft, inv, weights, traces, time_filter, midpoint_of, offset_of, shrink_level):
    n_mid = lax.axis_size("mid")
    n_freq = lax.axis_size("freq")
    n_off = lax.axis_size("off")
    sizes = (n_off, n_mid, n_freq)
    total = n_off * n_mid * n_freq
    me_mid = lax.axis_index("mid")
    me_off = lax.axis_index("off")
    tr_dev = traces.shape[1]
    count = shrink_level.shape[0] // (n_mid * n_off)
    width = 2 * count
    pack = max(1, min(tr_dev, 128 // width))
    n_traces = total * tr_dev
    n_mids = n_traces // NOFF
    f32, bf16 = jnp.float32, jnp.bfloat16

    if small(n_traces, n_off, n_mid, width):
        return fused(traces[0], time_filter, midpoint_of, offset_of, shrink_level, dft, inv, weights, sizes)[None]
    own_ids = midpoint_of * NOFF + offset_of
    filtered = jnp.dot(traces[0], time_filter, preferred_element_type=f32).astype(bf16)
    spectra = jnp.dot(filtered, dft, preferred_element_type=f32).astype(bf16)
    blocks = spectra.reshape(pack, tr_dev // pack, total, width)
    blocks = jnp.transpose(blocks, (2, 1, 0, 3)).reshape(total, tr_dev // pack, pack * width)
    own_levels = lax.dynamic_slice_in_dim(shrink_level, (me_mid * n_off + me_off) * count, count)
    level = jnp.broadcast_to(own_levels[:, None, None], (count, 1, NP))
    rows, ids = swap(blocks, sizes, 0, own_ids)
    rows = rows.reshape(total, tr_dev // pack, pack, width)
    rows = jnp.transpose(rows, (0, 2, 1, 3)).reshape(n_traces, width)
    cell_of = ids.reshape(n_traces)
    gather = jnp.zeros((n_traces, width), bf16).at[cell_of].set(rows)
    edged = jnp.pad(gather.reshape(n_mids, NOFF, 2, count).astype(f32), ((1, 1), (0, 0), (0, 0), (0, 0)))
    smooth = ((edged[:-2] + 2.0 * edged[1:-1] + edged[2:]) * 0.25).astype(bf16)
    smooth = jnp.transpose(smooth, (2, 3, 0, 1))
    mult = radon(smooth, level, weights, n_mid, n_off).reshape(width, n_traces)
    back = jnp.transpose(mult)[cell_of].reshape(total, pack, tr_dev // pack, width)
    back = jnp.transpose(back, (0, 2, 1, 3)).reshape(total, tr_dev // pack, pack * width)
    (returned,) = swap(back, sizes, 1)
    returned = returned.reshape(total, tr_dev // pack, pack, width)
    own_mult = jnp.transpose(returned, (2, 1, 0, 3)).reshape(tr_dev, total * width)
    clean = (spectra.astype(f32) - own_mult.astype(f32)).astype(bf16)
    sums = lax.dot_general(clean, dft, (((1,), (1,)), ((), ())), preferred_element_type=f32)
    return (2.0 * sums).astype(bf16)[None]


def solution(mesh):
    n_freq, n_mid, n_off = (mesh.shape[name] for name in ("freq", "mid", "off"))

    def run(traces, time_filter, midpoint_of, offset_of, shrink_level):
        n_freqs = shrink_level.shape[0]
        n_time = traces.shape[2]
        pieces = n_freq * n_mid * n_off
        count = n_freqs // pieces
        dft = dft_table(n_time, pieces, count).reshape(n_time, n_freq, n_mid, n_off, -1)
        weights = radon_table(n_freqs)
        part_traces = traces.shape[0] * traces.shape[1] // mesh.shape["group"]
        if small(part_traces, n_off, n_mid, 2 * count):
            dft = np.ascontiguousarray(dft[: n_time // 2].transpose(2, 0, 3, 1, 4)).reshape(n_mid, n_time // 2, -1)
            inv = np.ascontiguousarray(dft.transpose(0, 2, 1)) * np.asarray(2, dft.dtype)
            weights = weights.reshape(n_freqs // 2, 2, 2 * NOFF, NP).transpose(0, 2, 1, 3)
            weights = np.ascontiguousarray(weights).reshape(n_freqs // 2, 2 * NOFF, 2 * NP)
        else:
            dft = np.ascontiguousarray(dft.transpose(0, 3, 2, 1, 4)).reshape(n_time, 2 * n_freqs)
            inv = np.zeros((1,), dft.dtype)
        return jax.shard_map(
            on_device,
            mesh=mesh,
            in_specs=(
                P(),
                P(),
                P(),
                P("off", ("group", "mid", "freq"), None),
                P(),
                P("off", "group"),
                P("off", "group"),
                P("freq"),
            ),
            out_specs=P("off", ("group", "mid", "freq"), None),
            check_vma=False,
        )(jnp.asarray(dft), jnp.asarray(inv), jnp.asarray(weights), traces, time_filter, midpoint_of, offset_of, shrink_level)

    return run
```
